32 devices in a mesh: seq: 16 (over z, x, core), chan: 2 (over y).
Axes of the slice: x: 2, y: 2, z: 4, core: 2. Of those that a mesh axis runs over, the one named last changes fastest.
Arguments:
- hidden: bfloat16 [2, 8192, 2048], P(None, 'seq'), may hold values from -6 to 6
- nucleotides: int32 [8192], P('seq'), may hold values from 0 to 3
- base_embed: bfloat16 [4, 2048], replicated, may hold values from -6 to 6
- x_proj: bfloat16 [2048, 4096], P(None, 'chan'), may hold values from -0.125 to 0.125
- gate_proj: bfloat16 [2048, 4096], P(None, 'chan'), may hold values from -0.125 to 0.125
- bc_proj: bfloat16 [2048, 256], replicated, may hold values from -0.125 to 0.125
- conv_x: float32 [4, 4096], P(None, 'chan'), may hold values from -1.5 to 1.5
- bias_x: float32 [4096], P('chan'), may hold values from -0.35 to -0.15
- conv_bc: float32 [4, 256], replicated, may hold values from -1.5 to 1.5
- bias_bc: float32 [256], replicated, may hold values from -0.35 to -0.15
- log_decay: bfloat16 [2, 64, 8192], P(None, 'chan', 'seq'), may hold values from -1 to 0
- d_skip: float32 [64], P('chan'), may hold values from 0.1 to 0.4
- out_proj: bfloat16 [4096, 2048], P('chan'), may hold values from -0.5 to 0.5
Outputs:
- mixed: bfloat16 [2048, 8192], P('chan', 'seq')
The draws below stay inside these ranges and needn't reach their ends.
All inputs are finite; a program needn't handle non-finite values.
Results may differ from the reference program's by a relative error of at most 0.015.
Values may be sent and summed in bfloat16 or wider, within the bound.
A program may use at most 192 MiB of HBM per device.

```python
import math
import jax
import jax.numpy as jnp
from jax import lax

D = 2048
SSM_HEAD_COUNT = 64
HEAD_DIM = 64
NS = 128
KERNEL = 4
SPAN = 256
L_DEV = 512
E = 4096
SEQUENCE_LENGTH = 8192
N_CHAN = 2


def draw_log_decay(key, part):
    random_keys = jax.random.split(key, 5)
    share_fast = 0.5
    quick_heads = jax.random.uniform(random_keys[0], (2, SSM_HEAD_COUNT, 1)) < share_fast
    baseline_rate = jnp.where(quick_heads, 1.0 / 40.0, 0.4 / SEQUENCE_LENGTH)
    blocks = SEQUENCE_LENGTH // L_DEV
    multiplier = jnp.exp(jax.random.uniform(random_keys[1], (2, SSM_HEAD_COUNT, blocks), minval=math.log(0.5), maxval=math.log(2.0)))
    multiplier = jnp.repeat(multiplier, L_DEV, axis=2)
    noise_offset = jax.random.uniform(random_keys[2], (2, SSM_HEAD_COUNT, SEQUENCE_LENGTH), minval=0.5, maxval=1.5)
    spike_locations = jax.random.randint(random_keys[3], (2, SSM_HEAD_COUNT, 2, 1), 0, SEQUENCE_LENGTH)
    spike_drops = jax.random.uniform(random_keys[4], (2, SSM_HEAD_COUNT, 2, 1), minval=math.log(0.5), maxval=math.log(0.8))
    sequence_offsets = jnp.arange(SEQUENCE_LENGTH, dtype=jnp.int32)[None, None, None, :]
    spike_events = jnp.sum(jnp.where(sequence_offsets == spike_locations, spike_drops, 0.0), axis=2)
    drawn = jnp.clip(-baseline_rate * multiplier * noise_offset + spike_events, -1.0, 0.0)
    return drawn.astype(jnp.bfloat16)


def touch_ends(values, key, least, largest):
    longest = values.shape.index(max(values.shape))
    spots = []
    for shift in (0, 1):
        where = [jax.random.randint(jax.random.fold_in(key, axis), (), 0, length) for axis, length in enumerate(values.shape)]
        where[longest] = (where[longest] + shift) % values.shape[longest]
        spots.append(tuple(where))
    return values.at[spots[0]].set(least).at[spots[1]].set(largest)


def shard_levels(key, shape, shards, smallest, high):
    level = 1.0
    for dim, shards_of in shards:
        draws = jax.random.uniform(jax.random.fold_in(jax.random.fold_in(key, 6), dim), (shards_of,), jnp.float32, smallest / len(shards), high / len(shards))
        level = level * jnp.repeat(jnp.exp(draws), shape[dim] // shards_of).reshape((-1,) + (1,) * (len(shape) - 1 - dim))
    return level


def scatter_about(stream_key, extent, deviation, bound, shards=(), held_as=jnp.bfloat16):
    result = deviation * jax.random.normal(stream_key, extent, jnp.float32)
    if shards:
        result = result * shard_levels(stream_key, extent, shards, -0.22, 0.18)
    return jnp.clip(result, -bound, bound).astype(held_as)


def setup_inputs(seed: int = 0) -> dict:
    key_of = jax.random.split(jax.random.key(seed), 14)
    return {
        "hidden": scatter_about(key_of[0], (2, SEQUENCE_LENGTH, D), 1.0, 6.0, ((1, 16),)),
        "nucleotides": touch_ends(jax.random.randint(key_of[1], (SEQUENCE_LENGTH,), 0, 4), jax.random.fold_in(key_of[1], 1), 0, 3).astype(jnp.int32),
        "base_embed": scatter_about(key_of[2], (4, D), 1.0, 6.0),
        "x_proj": scatter_about(key_of[3], (D, E), D ** -0.5, 0.125, ((1, 2),)),
        "gate_proj": scatter_about(key_of[4], (D, E), D ** -0.5, 0.125, ((1, 2),)),
        "bc_proj": scatter_about(key_of[5], (D, 2 * NS), D ** -0.5, 0.125),
        "conv_x": scatter_about(key_of[6], (KERNEL, E), 0.25, 1.5, ((1, 2),), jnp.float32),
        "bias_x": jnp.clip(-0.35 + 0.19999999 * jax.random.uniform(key_of[7], (E,), jnp.float32) ** shard_levels(key_of[7], (E,), ((0, 2),), -0.2, 0.2), -0.35, -0.15),
        "conv_bc": scatter_about(key_of[8], (KERNEL, 2 * NS), 0.25, 1.5, (), jnp.float32),
        "bias_bc": jnp.clip(jax.random.uniform(key_of[9], (2 * NS,), jnp.float32, -0.35, -0.15), -0.35, -0.15),
        "log_decay": draw_log_decay(jax.random.fold_in(key_of[13], 71), 0),
        "d_skip": jnp.clip(0.1 + 0.3 * jax.random.uniform(key_of[11], (SSM_HEAD_COUNT,), jnp.float32) ** shard_levels(key_of[11], (SSM_HEAD_COUNT,), ((0, 2),), -0.2, 0.2), 0.1, 0.4),
        "out_proj": scatter_about(key_of[12], (E, D), (E // 32) ** -0.5, 0.5, ((0, 2),)),
    }


def strand_inputs(hidden_rows, id_rows, base_embed):
    id_codes = jnp.arange(4, dtype=jnp.int32)
    onehot = (id_rows[:, None] == id_codes[None, :]).astype(jnp.bfloat16)
    looked = jnp.dot(onehot, base_embed, preferred_element_type=jnp.float32)
    return (hidden_rows.astype(jnp.float32) + looked).astype(jnp.bfloat16)

def convolve(extended, conv_weight, conv_bias, length):
    conv_sum = conv_bias.astype(jnp.float32)
    for tap_index in range(conv_weight.shape[0]):
        conv_sum = conv_sum + conv_weight[tap_index] * extended[:, tap_index:tap_index + length].astype(jnp.float32)
    return jax.nn.silu(conv_sum).astype(jnp.bfloat16)

def block_scan(x_conv, b_rows, c_rows, rate_rows):
    strands, length, row_width = x_conv.shape
    head_count = rate_rows.shape[1]
    head_width = row_width // head_count
    state_width = b_rows.shape[-1]
    block_count = length // SPAN
    inv_root = state_width ** (-0.5)
    x_blocks = x_conv.reshape(strands, block_count, SPAN, head_count, head_width).transpose(1, 0, 2, 3, 4)
    b_blocks = b_rows.reshape(strands, block_count, SPAN, state_width).transpose(1, 0, 2, 3)
    c_blocks = c_rows.reshape(strands, block_count, SPAN, state_width).transpose(1, 0, 2, 3)
    g_blocks = rate_rows.reshape(strands, head_count, block_count, SPAN).transpose(2, 0, 1, 3)
    row_ids = lax.broadcasted_iota(jnp.int32, (SPAN, SPAN), 0)
    col_ids = lax.broadcasted_iota(jnp.int32, (SPAN, SPAN), 1)
    lower_mask = row_ids >= col_ids
    highest = lax.Precision.HIGHEST

    def block_step(carry_state, blk_args):
        x_blk, b_blk, c_blk, g_blk = blk_args
        cum_log = jnp.cumsum(g_blk, axis=-1)
        inject = jnp.sqrt(-jnp.expm1(2.0 * g_blk))
        scores = jnp.einsum('sqn,skn->sqk', c_blk.astype(jnp.float32), b_blk.astype(jnp.float32), precision=highest)
        log_gap = cum_log[..., :, None] - cum_log[..., None, :]
        decay_mask = jnp.where(lower_mask, jnp.exp(jnp.where(lower_mask, log_gap, 0.0)), 0.0)
        weights = (scores[:, None] * decay_mask * (inject * inv_root)[:, :, None, :]).astype(jnp.bfloat16)
        intra_term = jnp.einsum('shqk,skhp->sqhp', weights.astype(jnp.float32), x_blk.astype(jnp.float32), precision=highest)
        carried = jnp.einsum('sqn,shpn->sqhp', c_blk.astype(jnp.float32), carry_state, precision=highest)
        carried = carried * (jnp.exp(cum_log) * inv_root).transpose(0, 2, 1)[..., None]
        tail_scale = jnp.exp(cum_log[..., -1:] - cum_log) * inject
        scaled = x_blk.astype(jnp.float32) * tail_scale.transpose(0, 2, 1)[..., None]
        fresh_state = jnp.einsum('skhp,skn->shpn', scaled, b_blk.astype(jnp.float32), precision=highest)
        carry_state = jnp.exp(cum_log[..., -1])[..., None, None] * carry_state + fresh_state
        return (carry_state, intra_term + carried)
    zero_state = jnp.zeros((strands, head_count, head_width, state_width), jnp.float32)
    final_state, y_local = lax.scan(block_step, zero_state, (x_blocks, b_blocks, c_blocks, g_blocks))
    y_local = y_local.transpose(1, 0, 2, 3, 4).reshape(strands, length, head_count, head_width)
    return (y_local, final_state)

def reference(hidden, nucleotides, base_embed, x_proj, gate_proj, bc_proj, conv_x, bias_x, conv_bc, bias_bc, log_decay, d_skip, out_proj):
    strand_zero = strand_inputs(hidden[0], nucleotides, base_embed)
    strand_one = strand_inputs(hidden[1], 3 - nucleotides, base_embed)[::-1]
    inputs = jnp.stack([strand_zero, strand_one])
    rate_rows = jnp.stack([log_decay[0], log_decay[1][:, ::-1]]).astype(jnp.float32)
    flat_rows = inputs.reshape(2 * SEQUENCE_LENGTH, D)
    x_pre = jnp.dot(flat_rows, x_proj, preferred_element_type=jnp.float32).astype(jnp.bfloat16).reshape(2, SEQUENCE_LENGTH, E)
    z_pre = jnp.dot(flat_rows, gate_proj, preferred_element_type=jnp.float32).astype(jnp.bfloat16).reshape(2, SEQUENCE_LENGTH, E)
    bc_pre = jnp.dot(flat_rows, bc_proj, preferred_element_type=jnp.float32).astype(jnp.bfloat16).reshape(2, SEQUENCE_LENGTH, 2 * NS)
    kernel = conv_x.shape[0]
    x_ext = jnp.concatenate([jnp.zeros((2, kernel - 1, E), jnp.bfloat16), x_pre], axis=1)
    bc_ext = jnp.concatenate([jnp.zeros((2, kernel - 1, 2 * NS), jnp.bfloat16), bc_pre], axis=1)
    x_conv = convolve(x_ext, conv_x, bias_x, SEQUENCE_LENGTH)
    bc_conv = convolve(bc_ext, conv_bc, bias_bc, SEQUENCE_LENGTH)
    y_local, final_state = block_scan(x_conv, bc_conv[..., :NS], bc_conv[..., NS:], rate_rows)
    ssm = y_local + d_skip[None, None, :, None] * x_conv.reshape(2, SEQUENCE_LENGTH, SSM_HEAD_COUNT, HEAD_DIM).astype(jnp.float32)
    gated = (ssm.reshape(2, SEQUENCE_LENGTH, E) * jax.nn.silu(z_pre.astype(jnp.float32))).astype(jnp.bfloat16)
    forward_out = gated[0]
    reverse_out = gated[1][::-1]
    group_width = E // N_CHAN
    contract_dims = (((0,), (1,)), ((), ()))
    total_sum = jnp.zeros((D, SEQUENCE_LENGTH), jnp.float32)
    for group_index in range(N_CHAN):
        low = group_index * group_width
        w_rows = out_proj[low:low + group_width]
        part_sum = lax.dot_general(w_rows, forward_out[:, low:low + group_width], contract_dims, preferred_element_type=jnp.float32)
        part_sum = part_sum + lax.dot_general(w_rows, reverse_out[:, low:low + group_width], contract_dims, preferred_element_type=jnp.float32)
        part_sum = lax.optimization_barrier(part_sum.astype(jnp.bfloat16))
        total_sum = total_sum + part_sum.astype(jnp.float32)
    return total_sum.astype(jnp.bfloat16)
```

```python
import functools

import jax
import jax.numpy as jnp
from jax import lax
from jax.experimental import pallas as pl
from jax.experimental.pallas import tpu as pltpu
from jax.sharding import PartitionSpec as P

CHUNK = 128
WIDTH = 256
PAD = 16
LOG2E = 1.4426950408889634
MESH = pl.DeviceIdType.MESH


def silu(v):
    return v * (0.5 + 0.5 * jnp.tanh(0.5 * v))


def strand_inputs(hidden_rows, ids, base_embed):
    table = base_embed.astype(jnp.float32)
    pick = ids[:, None]
    low = jnp.where(pick == 0, table[0], table[1])
    high = jnp.where(pick == 2, table[2], table[3])
    looked = jnp.where(pick < 2, low, high)
    return (hidden_rows.astype(jnp.float32) + looked).astype(jnp.bfloat16)


def spread(cols, first, heads, head_dim):
    rows = cols.shape[0]
    per = 128 // head_dim
    lane = lax.broadcasted_iota(jnp.int32, (rows, 128), 1)
    tiles = []
    for t in range(heads // per):
        tile = jnp.broadcast_to(cols[:, first + t * per : first + t * per + 1], (rows, 128))
        for p in range(1, per):
            h = first + t * per + p
            tile = jnp.where(
                lane >= p * head_dim, jnp.broadcast_to(cols[:, h : h + 1], (rows, 128)), tile
            )
        tiles.append(tile)
    return jnp.concatenate(tiles, axis=1)


def state_kernel(head_dim, x_ref, rim_ref, taps_ref, bias_ref, tail_ref, decay_ref, bt_ref, conv_ref, state_ref, ext):
    strands, length, width = x_ref.shape
    taps = taps_ref.shape[0]
    heads = width // head_dim
    for s in range(strands):
        ext[8 : 8 + length] = x_ref[s].astype(jnp.float32)
        if s == 0:
            ext[0:8] = rim_ref[s].astype(jnp.float32)
        else:
            ext[8 + length : 16 + length] = rim_ref[s].astype(jnp.float32)
        chunks = length // CHUNK
        for step in range(chunks):
            c = step if s == 0 else chunks - 1 - step
            total = jnp.broadcast_to(bias_ref[...], (CHUNK, width))
            for k in range(taps):
                shift = k - (taps - 1) if s == 0 else (taps - 1) - k
                start = 8 + c * CHUNK + shift
                total = total + taps_ref[k : k + 1] * ext[start : start + CHUNK]
            rows = slice(c * CHUNK, (c + 1) * CHUNK)
            x = silu(total).astype(jnp.bfloat16)
            conv_ref[s, rows] = x
            scale = spread(tail_ref[0, rows], s * heads, heads, head_dim)
            xs = (x.astype(jnp.float32) * scale).astype(jnp.bfloat16)
            part = jnp.dot(bt_ref[s, :, rows], xs, preferred_element_type=jnp.float32)
            if step == 0:
                acc = part
            else:
                acc = acc + part
        states = acc.shape[0]
        state_ref[s, :states] = acc.astype(state_ref.dtype)
        state_ref[s, states:] = jnp.broadcast_to(
            decay_ref[s : s + 1], (PAD, width)
        ).astype(state_ref.dtype)


def scan_kernel(head_dim, s, x_ref, cols_ref, rows_ref, bt_ref, c_ref, chunk_ref, skip_ref, out_ref, scores):
    _, length, width = x_ref.shape
    heads = width // head_dim
    per = 128 // head_dim
    chunks = length // CHUNK

    @pl.when(pl.program_id(0) == 0)
    def _():
        t = lax.broadcasted_iota(jnp.int32, (CHUNK, CHUNK), 0)
        r = lax.broadcasted_iota(jnp.int32, (CHUNK, CHUNK), 1)
        keep = (r <= t) if s == 0 else (r >= t)
        for c in range(chunks):
            rows = slice(c * CHUNK, (c + 1) * CHUNK)
            sc = jnp.dot(c_ref[s, rows], bt_ref[s, :, rows], preferred_element_type=jnp.float32)
            scores[c] = jnp.where(keep, sc, 0.0)

    lane = lax.broadcasted_iota(jnp.int32, (CHUNK, 128), 1)
    state = None
    order = range(chunks) if s == 0 else range(chunks - 1, -1, -1)
    for step, c in enumerate(order):
        rows = slice(c * CHUNK, (c + 1) * CHUNK)
        cols = cols_ref[0, rows]
        base = s * 3 * heads
        x = x_ref[0, rows]
        sc = scores[c]
        y = skip_ref[...] * x.astype(jnp.float32)
        if step > 0:
            carried = jnp.dot(
                c_ref[s, rows], state.astype(jnp.bfloat16), preferred_element_type=jnp.float32
            )
            y = y + carried * spread(cols, base + heads, heads, head_dim)
        tiles = []
        for t in range(heads // per):
            xt = x[:, t * 128 : (t + 1) * 128]
            lhs, rhs = [], []
            for p in range(per):
                h = t * per + p
                gap = cols[:, base + h : base + h + 1] + rows_ref[0, s * heads + h : s * heads + h + 1, rows]
                lhs.append((sc * jnp.exp2(jnp.minimum(gap, 0.0))).astype(jnp.bfloat16))
                inside = (lane >= p * head_dim) & (lane < (p + 1) * head_dim)
                rhs.append(jnp.where(inside, xt, jnp.zeros_like(xt)))
            tiles.append(
                jnp.dot(
                    jnp.concatenate(lhs, axis=1),
                    jnp.concatenate(rhs, axis=0),
                    preferred_element_type=jnp.float32,
                )
            )
        y = y + jnp.concatenate(tiles, axis=1)
        out_ref[rows] = y.astype(out_ref.dtype)
        if step < chunks - 1:
            scale = spread(cols, base + 2 * heads, heads, head_dim)
            xs = (x.astype(jnp.float32) * scale).astype(jnp.bfloat16)
            fresh = jnp.dot(bt_ref[s, :, rows], xs, preferred_element_type=jnp.float32)
            at = s * chunks + c
            state = fresh if step == 0 else chunk_ref[at : at + 1] * state + fresh


def gate_kernel(head_dim, y_zero, y_one, z_ref, entry_ref, c_ref, in_ref, out_ref):
    strands, length, width = z_ref.shape
    y_refs = (y_zero, y_one)
    heads = width // head_dim
    for c in range(length // CHUNK):
        rows = slice(c * CHUNK, (c + 1) * CHUNK)
        total = 0.0
        for s in range(strands):
            carried = jnp.dot(c_ref[s, rows], in_ref[s], preferred_element_type=jnp.float32)
            y = y_refs[s][rows].astype(jnp.float32)
            y = y + carried * spread(entry_ref[0, rows], s * heads, heads, head_dim)
            total = total + y * silu(z_ref[s, rows].astype(jnp.float32))
        out_ref[rows] = total.astype(out_ref.dtype)


def neighbours(low_rows, high_rows):
    count = lax.axis_size("seq")
    forward = [(i, i + 1) for i in range(count - 1)]
    backward = [(i + 1, i) for i in range(count - 1)]
    return lax.ppermute(low_rows, "seq", forward), lax.ppermute(high_rows, "seq", backward)


def entering(local, states, across_work, line_work):
    count = lax.axis_size("seq")
    me = lax.axis_index("seq")
    half = local.shape[2] // 2
    core, across = me % 2, (me // 2) % 2
    row = lax.broadcasted_iota(jnp.int32, (1, local.shape[1], 1), 1)

    def decay(a):
        return a[..., states : states + 1, :].astype(jnp.float32)

    def joined(first, second, second_is_earlier):
        flag = second_is_earlier[:, None, None]
        a = jnp.where(flag, 1.0, decay(second))
        b = jnp.where(flag, decay(first), 1.0)
        first, second = first.astype(jnp.float32), second.astype(jnp.float32)
        both = jnp.where(row < states, a * first + b * second, first * second)
        return both.astype(jnp.bfloat16)

    def after(state, step, is_earlier):
        moved = decay(step) * state + step[..., :states, :].astype(jnp.float32)
        return jnp.where(is_earlier[:, None, None], moved, state)

    def mine(a):
        return lax.dynamic_slice_in_dim(a, core * half, half, a.ndim - 1)

    swap = [(i, i ^ 1) for i in range(count)]
    swap_pair = [(i, i ^ 2) for i in range(count)]
    up = [(i, i + 4) for i in range(count - 4)]
    down = [(i + 4, i) for i in range(count - 4)]

    other = lax.ppermute(local, "seq", swap)
    core_earlier = jnp.stack([core == 1, core == 0])
    chip = joined(mine(local), mine(other), core_earlier)
    chip_other = lax.ppermute(chip, "seq", swap_pair)
    results = []

    def beside(work, before, arrived):
        arrived, out = lax.optimization_barrier((arrived, work(before)))
        results.append(out)
        return arrived

    chip_other = beside(across_work, chip, chip_other)
    pair_earlier = jnp.stack([across == 1, across == 0])
    group = joined(chip, chip_other, pair_earlier)
    moving = [group[0], group[1]]
    total = [0.0, 0.0]
    factor = [1.0, 1.0]
    for step in range(count // 4 - 1):
        before = moving
        moving = [lax.ppermute(moving[0], "seq", up), lax.ppermute(moving[1], "seq", down)]
        if step < len(line_work):
            moving = beside(line_work[step], before, moving)
        for s in range(2):
            total[s] = total[s] + factor[s] * moving[s][:states].astype(jnp.float32)
            factor[s] = factor[s] * decay(moving[s])
    shape = (states, half)
    total = jnp.stack([jnp.broadcast_to(jnp.asarray(t, jnp.float32), shape) for t in total])
    chip_in = after(total, chip_other, pair_earlier).astype(jnp.bfloat16)
    rest = lax.ppermute(chip_in, "seq", swap)
    low = jnp.where(core == 0, chip_in, rest)
    high = jnp.where(core == 0, rest, chip_in)
    full = jnp.concatenate([low, high], axis=2).astype(jnp.float32)
    for work in line_work[max(count // 4 - 1, 0) :]:
        results.append(work(moving))
    return after(full, other, core_earlier).astype(jnp.bfloat16), results


def per_device(
    hidden, nucleotides, base_embed, x_proj, gate_proj, bc_proj, conv_x, bias_x, conv_bc,
    bias_bc, log_decay, d_skip, out_proj,
):
    taps, inner = conv_x.shape
    length = hidden.shape[1]
    head_count = d_skip.shape[0]
    head_dim = inner // head_count
    states = conv_bc.shape[1] // 2
    width = min(WIDTH, inner)
    blocks = inner // width
    heads = width // head_dim
    chunks = length // CHUNK
    inv_root = states ** (-0.5)

    r = jnp.arange(length)
    rates = log_decay.astype(jnp.float32)
    same = (r[:, None] // CHUNK) == (r[None, :] // CHUNK)
    older = [r[:, None] <= r[None, :], r[:, None] >= r[None, :]]

    def sums(masks):
        return jnp.stack(
            [
                jnp.dot(log_decay[s], masks[s].astype(jnp.bfloat16), preferred_element_type=jnp.float32)
                for s in range(2)
            ]
        )

    cum = sums([same & older[0], same & older[1]])
    left = sums([same & (r[:, None] > r[None, :]), same & (r[:, None] < r[None, :])])
    part = length // 2
    cum_all = sums(older)
    left_all = sums([r[:, None] > r[None, :], r[:, None] < r[None, :]])
    inject = jnp.sqrt(-jnp.expm1(2.0 * rates))
    tail_all = jnp.exp(left_all) * inject
    tail = jnp.exp(left) * inject
    entry = jnp.exp(cum) * inv_root
    row_terms = jnp.log2(inject * inv_root) - cum * LOG2E
    rows_arr = row_terms.reshape(2, blocks, heads, length).transpose(1, 0, 2, 3)
    rows_arr = rows_arr.reshape(blocks, 2 * heads, length)
    cols_arr = jnp.stack([cum * LOG2E, entry, tail], axis=1)
    cols_arr = cols_arr.reshape(2, 3, blocks, heads, length).transpose(2, 4, 0, 1, 3)
    cols_arr = cols_arr.reshape(blocks, length, 6 * heads)
    tail_arr = tail_all.reshape(2, blocks, heads, length).transpose(1, 3, 0, 2)
    tail_arr = tail_arr.reshape(blocks, length, 2 * heads)
    span_logs = jnp.sum(rates.reshape(2, head_count, chunks, CHUNK), axis=3)
    span_logs = jnp.repeat(span_logs.transpose(0, 2, 1), head_dim, axis=2)
    chunk_decay = jnp.exp(span_logs).reshape(2 * chunks, inner)
    shard_decay = jnp.exp(jnp.sum(span_logs, axis=1))
    entry_all = jnp.exp(cum_all) * inv_root
    entry_arr = entry_all.reshape(2, blocks, heads, length).transpose(1, 3, 0, 2)
    entry_arr = entry_arr.reshape(blocks, length, 2 * heads)
    skip = jnp.repeat(d_skip, head_dim)[None]

    inputs = jnp.concatenate(
        [
            strand_inputs(hidden[0], nucleotides, base_embed),
            strand_inputs(hidden[1], 3 - nucleotides, base_embed),
        ],
        axis=0,
    )
    inputs = lax.optimization_barrier(inputs)

    def project(weight):
        out = jnp.dot(inputs, weight, preferred_element_type=jnp.float32)
        return out.astype(jnp.bfloat16).reshape(2, length, -1)

    bc_pre = project(bc_proj)
    x_pre = project(x_proj)
    edge = taps - 1
    low = jnp.concatenate([x_pre[0, -edge:], bc_pre[0, -edge:]], axis=1)
    high = jnp.concatenate([x_pre[1, :edge], bc_pre[1, :edge]], axis=1)
    low, high = neighbours(low, high)
    x_rim = jnp.stack(
        [
            jnp.pad(low[:, :inner], ((8 - edge, 0), (0, 0))),
            jnp.pad(high[:, :inner], ((0, 8 - edge), (0, 0))),
        ]
    )
    bc_ext = [
        jnp.concatenate([low[:, inner:], bc_pre[0]], axis=0),
        jnp.concatenate([bc_pre[1], high[:, inner:]], axis=0),
    ]
    bc_conv = []
    for s in range(2):
        total = bias_bc
        for k in range(taps):
            at = k if s == 0 else edge - k
            total = total + conv_bc[k] * bc_ext[s][at : at + length].astype(jnp.float32)
        bc_conv.append(jax.nn.silu(total).astype(jnp.bfloat16))
    bc_conv = jnp.stack(bc_conv)
    c_rows = bc_conv[..., states:]
    b_cols = bc_conv[..., :states].transpose(0, 2, 1)

    params = pltpu.CompilerParams(dimension_semantics=("arbitrary",), vmem_limit_bytes=48 * 1024 * 1024)
    wide = pl.BlockSpec((2, length, width), lambda i: (0, 0, i))
    state_block = pl.BlockSpec((2, states, width), lambda i: (0, 0, i))
    whole = lambda a: pl.BlockSpec(a.shape, lambda i: (0,) * a.ndim)
    x_conv, local = pl.pallas_call(
        functools.partial(state_kernel, head_dim),
        grid=(blocks,),
        out_shape=(
            jax.ShapeDtypeStruct((2, length, inner), jnp.bfloat16),
            jax.ShapeDtypeStruct((2, states + PAD, inner), jnp.bfloat16),
        ),
        in_specs=[
            wide,
            pl.BlockSpec((2, 8, width), lambda i: (0, 0, i)),
            pl.BlockSpec((taps, width), lambda i: (0, i)),
            pl.BlockSpec((1, width), lambda i: (0, i)),
            pl.BlockSpec((1, length, 2 * heads), lambda i: (i, 0, 0)),
            pl.BlockSpec((2, width), lambda i: (0, i)),
            whole(b_cols),
        ],
        out_specs=(wide, pl.BlockSpec((2, states + PAD, width), lambda i: (0, 0, i))),
        scratch_shapes=[pltpu.VMEM((length + 16, width), jnp.float32)],
        compiler_params=params,
        name="conv_state",
    )(x_pre, x_rim, conv_x, bias_x[None], tail_arr, shard_decay, b_cols)

    def gate_rows(before):
        rows, _ = lax.optimization_barrier((inputs, before))
        out = jnp.dot(rows, gate_proj, preferred_element_type=jnp.float32)
        return out.astype(jnp.bfloat16).reshape(2, length, -1)

    def scan_strand(strand, before):
        x_in, _ = lax.optimization_barrier((x_conv, before))
        return pl.pallas_call(
        functools.partial(scan_kernel, head_dim, strand),
        grid=(blocks,),
        out_shape=jax.ShapeDtypeStruct((length, inner), jnp.bfloat16),
        in_specs=[
            pl.BlockSpec((1, length, width), lambda i: (strand, 0, i)),
            pl.BlockSpec((1, length, 6 * heads), lambda i: (i, 0, 0)),
            pl.BlockSpec((1, 2 * heads, length), lambda i: (i, 0, 0)),
            whole(b_cols),
            whole(c_rows),
            pl.BlockSpec((2 * chunks, width), lambda i: (0, i)),
            pl.BlockSpec((1, width), lambda i: (0, i)),
        ],
        out_specs=pl.BlockSpec((length, width), lambda i: (0, i)),
        scratch_shapes=[pltpu.VMEM((chunks, CHUNK, CHUNK), jnp.float32)],
        compiler_params=params,
        cost_estimate=pl.CostEstimate(
            flops=12 * length * inner * states, bytes_accessed=6 * length * inner, transcendentals=0
        ),
        name="scan",
    )(x_in, cols_arr, rows_arr, b_cols, c_rows, chunk_decay, skip)

    incoming, (z_pre, y_zero, y_one) = entering(
        local,
        states,
        gate_rows,
        [functools.partial(scan_strand, 0), functools.partial(scan_strand, 1)],
    )

    def scan_half(half, before=None):
        entered = incoming
        if before is not None:
            entered, _ = lax.optimization_barrier((incoming, before))
        rows_spec = pl.BlockSpec((2, part, width), lambda i: (0, half, i))
        return pl.pallas_call(
            functools.partial(gate_kernel, head_dim),
            grid=(blocks,),
            out_shape=jax.ShapeDtypeStruct((part, inner), jnp.bfloat16),
            in_specs=[
                pl.BlockSpec((part, width), lambda i: (half, i)),
                pl.BlockSpec((part, width), lambda i: (half, i)),
                rows_spec,
                pl.BlockSpec((1, part, 2 * heads), lambda i: (i, half, 0)),
                pl.BlockSpec((2, part, states), lambda i: (0, half, 0)),
                state_block,
            ],
            out_specs=pl.BlockSpec((part, width), lambda i: (0, i)),
            compiler_params=params,
            cost_estimate=pl.CostEstimate(
                flops=96 * part * inner * states, bytes_accessed=48 * part * inner, transcendentals=0
            ),
            name="gate",
        )(y_zero, y_one, z_pre, entry_arr, c_rows, entered)

    def out_part(weight, rows):
        return lax.dot_general(
            weight, rows, (((0,), (1,)), ((), ())), preferred_element_type=jnp.float32
        ).astype(jnp.bfloat16)

    if lax.axis_size("chan") == 2:
        size = out_proj.shape[1] // 2
        mine = lax.axis_index("chan")
        send_weight = lax.dynamic_slice_in_dim(out_proj, (1 - mine) * size, size, 1)
        own_weight = lax.dynamic_slice_in_dim(out_proj, mine * size, size, 1)
        first = scan_half(0)
        part_first = out_part(send_weight, first)
        sent_first = lax.ppermute(part_first, "chan", [(0, 1), (1, 0)])
        second = scan_half(1, part_first)
        sent_first, second = lax.optimization_barrier((sent_first, second))
        sent_second = lax.ppermute(out_part(send_weight, second), "chan", [(0, 1), (1, 0)])
        own = lax.optimization_barrier(out_part(own_weight, jnp.concatenate([first, second])))
        sent = jnp.concatenate([sent_first, sent_second], axis=1)
        return (own.astype(jnp.float32) + sent.astype(jnp.float32)).astype(jnp.bfloat16)
    mixed_in = jnp.concatenate([scan_half(0), scan_half(1)])
    return lax.psum_scatter(
        out_part(out_proj, mixed_in), "chan", scatter_dimension=0, tiled=True
    )


GROUP = 128
SUB = 64
HALO = 16
BLOCK = 256


def split_store(ref, s, rows, value, heads):
    high = value.astype(jnp.bfloat16)
    ref[s, rows, 0:heads] = high
    ref[s, rows, heads : 2 * heads] = (value - high.astype(jnp.float32)).astype(jnp.bfloat16)


def one_minus_exp(u):
    small = -u * (1 + u / 2 * (1 + u / 3 * (1 + u / 4 * (1 + u / 5 * (1 + u / 6)))))
    return jnp.where(u > -0.25, small, 1.0 - jnp.exp(u))


def nt(a, b):
    return lax.dot_general(a, b, (((1,), (1,)), ((), ())), preferred_element_type=jnp.float32)


def mm(a, b):
    return jnp.dot(a, b, preferred_element_type=jnp.float32)


def layer_kernel(
    head_dim, ids_ref, hid_ref, emb_ref, wx_hbm, wz_hbm, wbc_hbm, wo_hbm, tapx_ref, biasx_ref, tapbc_ref, biasbc_ref,
    ld_ref, skip_ref, out_ref,
    a_buf, w_buf, wz_buf, wbc_buf, ext, x_buf, xs_buf, st_buf, lh_buf, bt_buf, g_col, f_col, e_col, r_row,
    ids_low, ids_high, loc, core_in, chip, x_in, grp, grp_dec, z_out, z_in, ent_out, entry, a_cat, gated, y_out, y_in, own,
    load_sem, wx_sem, halo_s, halo_r, core_s, core_r, x_s, x_r, z_s, z_r, ent_s, ent_r, y_s, y_r,
):
    _, length, depth = hid_ref.shape
    inner = wx_hbm.shape[1]
    feats = wo_hbm.shape[1] // 2
    taps = tapx_ref.shape[0]
    heads = inner // head_dim
    states = tapbc_ref.shape[1] // 2
    blocks = inner // BLOCK
    half = BLOCK // 2
    groups = length // GROUP
    subs = length // SUB
    inv_root = states ** (-0.5)
    bf, f32 = jnp.bfloat16, jnp.float32
    starts = (HALO, HALO + length)

    count = lax.axis_size("seq")
    me = lax.axis_index("seq")
    lane_mate = lax.axis_index("chan")
    core, across, line = me % 2, (me // 2) % 2, me // 4
    lines = count // 4
    right, left = (me + 1) % count, (me + count - 1) % count
    mate = me + 1 - 2 * core
    side = me + 2 - 4 * across
    up, down = (me + 4) % count, (me + count - 4) % count
    other_chan = 1 - lane_mate

    loads = [
        pltpu.make_async_copy(hid_ref.at[0], a_buf.at[pl.ds(starts[0], length)], load_sem.at[0]),
        pltpu.make_async_copy(hid_ref.at[1], a_buf.at[pl.ds(starts[1], length)], load_sem.at[1]),
        pltpu.make_async_copy(wbc_hbm, wbc_buf, load_sem.at[2]),
    ]

    def wx_load(j):
        cols = pl.ds(pl.multiple_of(j * BLOCK, BLOCK), BLOCK)
        return pltpu.make_async_copy(wx_hbm.at[:, cols], w_buf.at[:, cols], wx_sem.at[j])

    wz_load = pltpu.make_async_copy(wz_hbm, wz_buf, load_sem.at[3])
    wo_load = pltpu.make_async_copy(wo_hbm, w_buf, load_sem.at[4])
    for c in loads:
        c.start()
    for j in range(blocks):
        wx_load(j).start()
    wz_load.start()

    barrier = pltpu.get_barrier_semaphore()
    for peer in (right, left, mate, side, up, down):
        pl.semaphore_signal(barrier, inc=1, device_id={"seq": peer}, device_id_type=MESH)
    pl.semaphore_signal(barrier, inc=1, device_id={"chan": other_chan}, device_id_type=MESH)
    pl.semaphore_wait(barrier, 7)

    def send(src, dst, s_sem, r_sem, **where):
        return pltpu.make_async_remote_copy(
            src_ref=src, dst_ref=dst, send_sem=s_sem, recv_sem=r_sem, device_id=where, device_id_type=MESH
        )

    halos = [
        send(hid_ref.at[0, pl.ds(length - HALO, HALO)], a_buf.at[pl.ds(0, HALO)], halo_s.at[0], halo_r.at[0], seq=right),
        send(hid_ref.at[1, pl.ds(0, HALO)], a_buf.at[pl.ds(HALO + 2 * length, HALO)], halo_s.at[1], halo_r.at[1], seq=left),
        send(ids_ref, ids_low, halo_s.at[2], halo_r.at[2], seq=right),
        send(ids_ref, ids_high, halo_s.at[3], halo_r.at[3], seq=left),
    ]
    for c in halos:
        c.start()

    t = lax.broadcasted_iota(jnp.int32, (GROUP, GROUP), 0)
    r = lax.broadcasted_iota(jnp.int32, (GROUP, GROUP), 1)
    same = (t // SUB) == (r // SUB)
    low_half = (r % SUB) < (SUB // 2)
    older = (r <= t, r >= t)
    first_half = (low_half, jnp.logical_not(low_half))
    eye = (t == r).astype(f32)
    row = lax.broadcasted_iota(jnp.int32, (32, length), 0)
    pos = lax.broadcasted_iota(jnp.int32, (32, length), 1)
    row_id = lax.broadcasted_iota(jnp.int32, (32, heads), 0)
    in_sub = ((pos // SUB) == (row % 8)).astype(f32)
    in_low = ((pos % SUB) < (SUB // 2)).astype(f32)
    for s in range(2):
        q_mask = jnp.where(same, older[s].astype(f32) - first_half[s].astype(f32), 0.0)
        masks = jnp.concatenate([q_mask, older[s].astype(f32), eye], axis=0).astype(bf)
        before = jnp.zeros((1, heads), f32)
        for g in range(groups) if s == 0 else range(groups - 1, -1, -1):
            rows = slice(g * GROUP, (g + 1) * GROUP)
            res = nt(masks, ld_ref[s, :, rows])
            q, cum, rate = res[0:GROUP], res[GROUP : 2 * GROUP], res[2 * GROUP :]
            inject = jnp.sqrt(one_minus_exp(2.0 * rate))
            split_store(g_col, s, rows, jnp.exp(-q) * inject, heads)
            split_store(f_col, s, rows, jnp.exp(q) * inv_root, heads)
            cum = cum + before
            split_store(e_col, s, rows, jnp.exp(cum) * inv_root, heads)
            before = cum[GROUP - 1 :] if s == 0 else cum[0:1]
        first = in_low if s == 0 else 1.0 - in_low
        kind = row // 8
        pick = jnp.where(kind == 0, first, jnp.where(kind == 1, 1.0 - first, 1.0)) * in_sub
        pick = jnp.where(row == 24, 1.0, pick)
        logs = nt(pick.astype(bf), ld_ref[s])
        split_store(r_row, s, slice(0, 32), jnp.where(row_id == 25, skip_ref[...], jnp.exp(logs)), heads)

    code = lax.broadcasted_iota(jnp.int32, (8, GROUP), 0)
    table = jnp.concatenate([emb_ref[...].astype(f32), jnp.zeros((4, depth), f32)], axis=0).astype(bf)

    def looked(ids, flip):
        ids = 3 - ids if flip else ids
        n = ids.shape[1]
        hot = (code[:, :n] == jnp.broadcast_to(ids, (8, n))).astype(f32)
        return hot.T.astype(bf)

    for s in range(2):
        loads[s].wait()
        for g in range(groups):
            hot = looked(ids_ref[:, g * GROUP : (g + 1) * GROUP], s == 1)
            rows = slice(starts[s] + g * GROUP, starts[s] + (g + 1) * GROUP)
            a_buf[rows] = (a_buf[rows].astype(f32) + mm(hot, table)).astype(bf)
    for c in halos:
        c.wait()
    hot = looked(ids_low[:, length - GROUP :], False)[GROUP - HALO :]
    rows = slice(0, HALO)
    a_buf[rows] = jnp.where(me > 0, a_buf[rows].astype(f32) + mm(hot, table), 0.0).astype(bf)
    hot = looked(ids_high[:, :GROUP], True)[:HALO]
    rows = slice(HALO + 2 * length, 2 * HALO + 2 * length)
    a_buf[rows] = jnp.where(me < count - 1, a_buf[rows].astype(f32) + mm(hot, table), 0.0).astype(bf)

    def conv(s, g, tap_rows, bias):
        total = jnp.broadcast_to(bias, (GROUP, BLOCK))
        for k in range(taps):
            shift = k - (taps - 1) if s == 0 else (taps - 1) - k
            start = starts[s] + g * GROUP + shift
            total = total + tap_rows[k : k + 1] * ext[start : start + GROUP]
        return silu(total)

    loads[2].wait()
    ext[...] = mm(a_buf[...], wbc_buf[...]).astype(bf).astype(f32)
    for s in range(2):
        keep = same & older[s]
        for g in range(groups):
            rows = slice(g * GROUP, (g + 1) * GROUP)
            both = conv(s, g, tapbc_ref[...], biasbc_ref[...])
            b, c = both[:, :states].astype(bf), both[:, states:].astype(bf)
            lh_buf[s, rows, 0:states] = c
            lh_buf[s, rows, states : states + GROUP] = jnp.where(keep, nt(c, b), 0.0).astype(bf)
            bt = b.astype(f32).T
            lower = r < SUB
            bt_buf[s, g, 0:states] = jnp.where(lower, bt, 0.0).astype(bf)
            bt_buf[s, g, states : 2 * states] = jnp.where(lower, 0.0, bt).astype(bf)

    head_row = lax.broadcasted_iota(jnp.int32, (2 * heads, BLOCK), 0) % heads
    head_lane = lax.broadcasted_iota(jnp.int32, (2 * heads, BLOCK), 1) // head_dim

    def spreader(j):
        return (head_row == head_lane + j * (BLOCK // head_dim)).astype(f32).astype(bf)

    def columns(j):
        return pl.ds(pl.multiple_of(j * BLOCK, BLOCK), BLOCK)

    def decay_of(a):
        return a[states : states + 1].astype(f32) + a[states + 1 : states + 2].astype(f32)

    def state_of(a):
        return a[0:states].astype(f32)

    def put(ref, at, s, state, decay):
        ref[at, s, 0:states] = state.astype(bf)
        high = decay.astype(bf)
        low = decay - high.astype(f32)
        pad_row = lax.broadcasted_iota(jnp.int32, (PAD, half), 0)
        ref[at, s, states : states + PAD] = jnp.where(pad_row == 0, high.astype(f32), low).astype(bf)

    def core_copy(b):
        return send(loc.at[b * 2 + 1 - core], core_in.at[b], core_s.at[b], core_r.at[b], seq=mate)

    def x_copy(b):
        return send(chip.at[b], x_in.at[b], x_s.at[b], x_r.at[b], seq=side)

    def z_copy(b, s):
        return send(z_out.at[b, s], z_in.at[b, s], z_s.at[b, s], z_r.at[b, s], seq=up if s == 0 else down)

    def ent_copy(b):
        span = pl.ds(pl.multiple_of(core * half, half), half)
        return send(ent_out.at[b], entry.at[b, :, :, span], ent_s.at[b], ent_r.at[b], seq=mate)

    def ent_arrived(b):
        span = pl.ds(pl.multiple_of((1 - core) * half, half), half)
        return send(ent_out.at[b], entry.at[b, :, :, span], ent_s.at[b], ent_r.at[b], seq=mate)

    def join(first, second, swapped):
        d1, d2 = decay_of(first), decay_of(second)
        s1, s2 = state_of(first), state_of(second)
        scale = jnp.where(swapped, d1, d2)
        state = jnp.where(swapped, scale * s2 + s1, scale * s1 + s2)
        return state, d1 * d2

    def chip_stage(b):
        core_copy(b).wait_recv()
        for s in range(2):
            mine, other = loc[b * 2 + core, s], core_in[b, s]
            swapped = (core == 1) if s == 0 else (core == 0)
            state, decay = join(mine, other, swapped)
            put(chip, b, s, state, decay)
        x_copy(b).start()

    def group_stage(b):
        x_copy(b).wait_recv()
        for s in range(2):
            swapped = (across == 1) if s == 0 else (across == 0)
            state, decay = join(chip[b, s], x_in[b, s], swapped)
            grp[b, s] = state
            grp_dec[b, s] = jnp.broadcast_to(decay, (8, half))
            z_out[b, s] = state.astype(bf)

            @pl.when(line == (0 if s == 0 else lines - 1))
            def _():
                z_copy(b, s).start()

    def line_stage(b, k):
        for s in range(2):
            at = k if s == 0 else lines - 1 - k

            @pl.when(line == at)
            def _():
                z_copy(b, s).wait_recv()
                if k < lines - 1:
                    state = grp_dec[b, s][0:1] * z_in[b, s].astype(f32) + grp[b, s]
                    z_out[b, s] = state.astype(bf)
                    z_copy(b, s).start()

    def enter_stage(b):
        for s in range(2):
            edge = line == (0 if s == 0 else lines - 1)
            entering = jnp.where(edge, 0.0, z_in[b, s].astype(f32))
            later_chip = (across == 1) if s == 0 else (across == 0)
            past = x_in[b, s]
            entering = jnp.where(later_chip, decay_of(past) * entering + state_of(past), entering)
            first = (core == 0) if s == 0 else (core == 1)
            mine, other = loc[b * 2 + core, s], core_in[b, s]
            dec = jnp.where(first, decay_of(mine), decay_of(other))
            adds = jnp.where(first, state_of(mine), state_of(other))
            second = dec * entering + adds
            span = pl.ds(pl.multiple_of(core * half, half), half)
            entry[b, s, :, span] = jnp.where(first, entering, second).astype(bf)
            ent_out[b, s] = jnp.where(first, second, entering).astype(bf)
        ent_copy(b).start()

    stages = [chip_stage, group_stage]
    stages += [functools.partial(line_stage, k=k) for k in range(1, lines)]
    stages += [enter_stage]

    def exchange(at):
        for lag, stage in enumerate(stages):
            b = at - 1 - lag

            @pl.when((b >= 0) & (b < blocks))
            def _():
                stage(b)

    def local_states(j, _):
        wx_load(j).wait()
        cols = columns(j)
        ext[...] = mm(a_buf[...], w_buf[:, cols]).astype(bf).astype(f32)
        exchange(j)
        spread_to = spreader(j)
        tap_rows, bias = tapx_ref[:, cols], biasx_ref[:, cols]
        for s in range(2):
            rows_at = mm(r_row[s], spread_to)
            state = None
            for g in range(groups) if s == 0 else range(groups - 1, -1, -1):
                rows = slice(g * GROUP, (g + 1) * GROUP)
                x = conv(s, g, tap_rows, bias).astype(bf)
                x_buf[s, rows, cols] = x
                xs = (x.astype(f32) * mm(g_col[s, rows], spread_to)).astype(bf)
                xs_buf[s, rows, cols] = xs
                fresh = mm(bt_buf[s, g], xs)
                for p in (0, 1) if s == 0 else (1, 0):
                    c = 2 * g + p
                    part = rows_at[8 + c : 9 + c] * fresh[p * states : (p + 1) * states]
                    if state is None:
                        st_buf[s, c, :, cols] = jnp.zeros((states, BLOCK), bf)
                        state = part
                    else:
                        st_buf[s, c, :, cols] = (state * rows_at[c : c + 1]).astype(bf)
                        state = rows_at[16 + c : 17 + c] * state + part
            for p in range(2):
                lanes = slice(p * half, (p + 1) * half)
                put(loc, j * 2 + p, s, state[:, lanes], rows_at[24:25, lanes])
        core_copy(j).start()
        return 0

    lax.fori_loop(0, blocks, local_states, 0)
    wo_load.start()

    def local_outputs(j, _):
        exchange(j + blocks)
        cols = columns(j)
        spread_to = spreader(j)
        for s in range(2):
            skip = mm(r_row[s], spread_to)[25:26]
            for g in range(groups):
                rows = slice(g * GROUP, (g + 1) * GROUP)
                factor = mm(f_col[s, rows], spread_to)
                xs = xs_buf[s, rows, cols]
                x = x_buf[s, rows, cols].astype(f32)
                ys = []
                for p in range(2):
                    c = 2 * g + p
                    rhs = jnp.concatenate([st_buf[s, c, :, cols], xs], axis=0)
                    ys.append(mm(lh_buf[s, c * SUB : (c + 1) * SUB], rhs))
                y = jnp.concatenate(ys, axis=0) * factor + skip * x
                x_buf[s, rows, cols] = y.astype(bf)
        return 0

    lax.fori_loop(0, blocks, local_outputs, 0)

    for at in range(2 * blocks, blocks + len(stages) + 1):
        exchange(jnp.int32(at))
    for b in range(blocks):
        ent_arrived(b).wait_recv()
    wz_load.wait()
    wo_load.wait()

    def y_copy(i):
        return send(y_out.at[i], y_in.at[i], y_s.at[i], y_r.at[i], chan=other_chan)

    def rows_out(i, _):
        for s in range(2):
            rows = pl.ds(pl.multiple_of(starts[s] + i * GROUP, 16), GROUP)
            a_cat[s * GROUP : (s + 1) * GROUP] = a_buf[rows]
        rows = pl.ds(pl.multiple_of(i * GROUP, GROUP), GROUP)

        def gate(j, _):
            cols = columns(j)
            spread_to = spreader(j)
            z = silu(mm(a_cat[...], wz_buf[:, cols]).astype(bf).astype(f32))
            total = 0.0
            for s in range(2):
                carried = mm(lh_buf[s, rows, 0:states], entry[j, s])
                y = x_buf[s, rows, cols].astype(f32) + carried * mm(e_col[s, rows], spread_to)
                total = total + y * z[s * GROUP : (s + 1) * GROUP]
            gated[:, cols] = total.astype(bf)
            return 0

        lax.fori_loop(0, blocks, gate, 0)

        def project(chan, target):
            def step(n, _):
                at = pl.ds(pl.multiple_of(n * BLOCK, BLOCK), BLOCK)
                cols = pl.ds(pl.multiple_of(chan * feats + n * BLOCK, BLOCK), BLOCK)
                target[i, :, at] = mm(gated[...], w_buf[:, cols]).astype(bf)
                return 0

            lax.fori_loop(0, feats // BLOCK, step, 0)

        project(other_chan, y_out)
        y_copy(i).start()
        project(lane_mate, own)
        return 0

    lax.fori_loop(0, groups, rows_out, 0)

    for i in range(groups):
        y_copy(i).wait_recv()
        rows = slice(i * GROUP, (i + 1) * GROUP)
        out_ref[rows] = (own[i].astype(f32) + y_in[i].astype(f32)).astype(bf)

    for i in range(groups):
        y_copy(i).wait_send()
    for b in range(blocks):
        core_copy(b).wait_send()
        x_copy(b).wait_send()
        ent_copy(b).wait_send()

    @pl.when(line < lines - 1)
    def _():
        for b in range(blocks):
            z_copy(b, 0).wait_send()

    @pl.when(line > 0)
    def _():
        for b in range(blocks):
            z_copy(b, 1).wait_send()


def fused_device(
    hidden, nucleotides, base_embed, x_proj, gate_proj, bc_proj, conv_x, bias_x, conv_bc,
    bias_bc, log_decay, d_skip, out_proj,
):
    length, depth = hidden.shape[1:]
    inner = x_proj.shape[1]
    feats = out_proj.shape[1] // 2
    heads = d_skip.shape[0]
    states = conv_bc.shape[1] // 2
    blocks, groups, subs, half = inner // BLOCK, length // GROUP, length // SUB, BLOCK // 2
    rows = 2 * length + 2 * HALO
    bf, f32 = jnp.bfloat16, jnp.float32
    vmem, dma = pltpu.VMEM, pltpu.SemaphoreType.DMA
    small = pl.BlockSpec(memory_space=pltpu.VMEM)
    large = pl.BlockSpec(memory_space=pl.ANY)
    pair = (blocks, 2, states + PAD, half)
    out = pl.pallas_call(
        functools.partial(layer_kernel, inner // heads),
        out_shape=jax.ShapeDtypeStruct((length, feats), bf),
        in_specs=[small, large, small, large, large, large, large] + [small] * 6,
        out_specs=small,
        scratch_shapes=[
            vmem((rows, depth), bf),
            vmem((depth, inner), bf),
            vmem((depth, inner), bf),
            vmem((depth, 2 * states), bf),
            vmem((rows, BLOCK), f32),
            vmem((2, length, inner), bf),
            vmem((2, length, inner), bf),
            vmem((2, subs, states, inner), bf),
            vmem((2, length, states + GROUP), bf),
            vmem((2, groups, 2 * states, GROUP), bf),
            vmem((2, length, 2 * heads), bf),
            vmem((2, length, 2 * heads), bf),
            vmem((2, length, 2 * heads), bf),
            vmem((2, 32, 2 * heads), bf),
            vmem((1, length), jnp.int32),
            vmem((1, length), jnp.int32),
            vmem((2 * blocks, 2, states + PAD, half), bf),
            vmem(pair, bf),
            vmem(pair, bf),
            vmem(pair, bf),
            vmem((blocks, 2, states, half), f32),
            vmem((blocks, 2, 8, half), f32),
            vmem((blocks, 2, states, half), bf),
            vmem((blocks, 2, states, half), bf),
            vmem((blocks, 2, states, half), bf),
            vmem((blocks, 2, states, BLOCK), bf),
            vmem((2 * GROUP, depth), bf),
            vmem((GROUP, inner), bf),
            vmem((groups, GROUP, feats), bf),
            vmem((groups, GROUP, feats), bf),
            vmem((groups, GROUP, feats), bf),
            dma((5,)), dma((blocks,)), dma((4,)), dma((4,)),
            dma((blocks,)), dma((blocks,)), dma((blocks,)), dma((blocks,)),
            dma((blocks, 2)), dma((blocks, 2)), dma((blocks,)), dma((blocks,)),
            dma((groups,)), dma((groups,)),
        ],
        compiler_params=pltpu.CompilerParams(
            collective_id=0, has_side_effects=True, vmem_limit_bytes=67043328
        ),
        name="layer",
    )(
        nucleotides[None], hidden, base_embed, x_proj, gate_proj, bc_proj, out_proj, conv_x, bias_x[None], conv_bc,
        bias_bc[None], log_decay, d_skip[None],
    )
    return out.T


def any_device(*args):
    hidden, x_proj, conv_bc = args[0], args[3], args[8]
    fits = lax.axis_size("chan") == 2 and lax.axis_size("seq") % 4 == 0 and lax.axis_size("seq") >= 8
    fits = fits and hidden.shape[1] == 8 * SUB and conv_bc.shape[1] == BLOCK and x_proj.shape[1] % BLOCK == 0
    return fused_device(*args) if fits else per_device(*args)


def solution(mesh):
    in_specs = (
        P(None, "seq", None), P("seq"), P(), P(None, "chan"), P(None, "chan"), P(),
        P(None, "chan"), P("chan"), P(), P(), P(None, "chan", "seq"), P("chan"), P("chan", None),
    )
    return jax.shard_map(
        any_device, mesh=mesh, in_specs=in_specs, out_specs=P("chan", "seq"), check_vma=False
    )
```

```python
import functools

import jax
import jax.numpy as jnp
from jax import lax
from jax.experimental import pallas as pl
from jax.experimental.pallas import tpu as pltpu
from jax.sharding import PartitionSpec as P

CHUNK = 128
WIDTH = 256
PAD = 16
LOG2E = 1.4426950408889634
MESH = pl.DeviceIdType.MESH


def silu(v):
    return v * (0.5 + 0.5 * jnp.tanh(0.5 * v))


def strand_inputs(hidden_rows, ids, base_embed):
    table = base_embed.astype(jnp.float32)
    pick = ids[:, None]
    low = jnp.where(pick == 0, table[0], table[1])
    high = jnp.where(pick == 2, table[2], table[3])
    looked = jnp.where(pick < 2, low, high)
    return (hidden_rows.astype(jnp.float32) + looked).astype(jnp.bfloat16)


def spread(cols, first, heads, head_dim):
    rows = cols.shape[0]
    per = 128 // head_dim
    lane = lax.broadcasted_iota(jnp.int32, (rows, 128), 1)
    tiles = []
    for t in range(heads // per):
        tile = jnp.broadcast_to(cols[:, first + t * per : first + t * per + 1], (rows, 128))
        for p in range(1, per):
            h = first + t * per + p
            tile = jnp.where(
                lane >= p * head_dim, jnp.broadcast_to(cols[:, h : h + 1], (rows, 128)), tile
            )
        tiles.append(tile)
    return jnp.concatenate(tiles, axis=1)


def state_kernel(head_dim, x_ref, rim_ref, taps_ref, bias_ref, tail_ref, decay_ref, bt_ref, conv_ref, state_ref, ext):
    strands, length, width = x_ref.shape
    taps = taps_ref.shape[0]
    heads = width // head_dim
    for s in range(strands):
        ext[8 : 8 + length] = x_ref[s].astype(jnp.float32)
        if s == 0:
            ext[0:8] = rim_ref[s].astype(jnp.float32)
        else:
            ext[8 + length : 16 + length] = rim_ref[s].astype(jnp.float32)
        chunks = length // CHUNK
        for step in range(chunks):
            c = step if s == 0 else chunks - 1 - step
            total = jnp.broadcast_to(bias_ref[...], (CHUNK, width))
            for k in range(taps):
                shift = k - (taps - 1) if s == 0 else (taps - 1) - k
                start = 8 + c * CHUNK + shift
                total = total + taps_ref[k : k + 1] * ext[start : start + CHUNK]
            rows = slice(c * CHUNK, (c + 1) * CHUNK)
            x = silu(total).astype(jnp.bfloat16)
            conv_ref[s, rows] = x
            scale = spread(tail_ref[0, rows], s * heads, heads, head_dim)
            xs = (x.astype(jnp.float32) * scale).astype(jnp.bfloat16)
            part = jnp.dot(bt_ref[s, :, rows], xs, preferred_element_type=jnp.float32)
            if step == 0:
                acc = part
            else:
                acc = acc + part
        states = acc.shape[0]
        state_ref[s, :states] = acc.astype(state_ref.dtype)
        state_ref[s, states:] = jnp.broadcast_to(
            decay_ref[s : s + 1], (PAD, width)
        ).astype(state_ref.dtype)


def scan_kernel(head_dim, s, x_ref, cols_ref, rows_ref, bt_ref, c_ref, chunk_ref, skip_ref, out_ref, scores):
    _, length, width = x_ref.shape
    heads = width // head_dim
    per = 128 // head_dim
    chunks = length // CHUNK

    @pl.when(pl.program_id(0) == 0)
    def _():
        t = lax.broadcasted_iota(jnp.int32, (CHUNK, CHUNK), 0)
        r = lax.broadcasted_iota(jnp.int32, (CHUNK, CHUNK), 1)
        keep = (r <= t) if s == 0 else (r >= t)
        for c in range(chunks):
            rows = slice(c * CHUNK, (c + 1) * CHUNK)
            sc = jnp.dot(c_ref[s, rows], bt_ref[s, :, rows], preferred_element_type=jnp.float32)
            scores[c] = jnp.where(keep, sc, 0.0)

    lane = lax.broadcasted_iota(jnp.int32, (CHUNK, 128), 1)
    state = None
    order = range(chunks) if s == 0 else range(chunks - 1, -1, -1)
    for step, c in enumerate(order):
        rows = slice(c * CHUNK, (c + 1) * CHUNK)
        cols = cols_ref[0, rows]
        base = s * 3 * heads
        x = x_ref[0, rows]
        sc = scores[c]
        y = skip_ref[...] * x.astype(jnp.float32)
        if step > 0:
            carried = jnp.dot(
                c_ref[s, rows], state.astype(jnp.bfloat16), preferred_element_type=jnp.float32
            )
            y = y + carried * spread(cols, base + heads, heads, head_dim)
        tiles = []
        for t in range(heads // per):
            xt = x[:, t * 128 : (t + 1) * 128]
            lhs, rhs = [], []
            for p in range(per):
                h = t * per + p
                gap = cols[:, base + h : base + h + 1] + rows_ref[0, s * heads + h : s * heads + h + 1, rows]
                lhs.append((sc * jnp.exp2(jnp.minimum(gap, 0.0))).astype(jnp.bfloat16))
                inside = (lane >= p * head_dim) & (lane < (p + 1) * head_dim)
                rhs.append(jnp.where(inside, xt, jnp.zeros_like(xt)))
            tiles.append(
                jnp.dot(
                    jnp.concatenate(lhs, axis=1),
                    jnp.concatenate(rhs, axis=0),
                    preferred_element_type=jnp.float32,
                )
            )
        y = y + jnp.concatenate(tiles, axis=1)
        out_ref[rows] = y.astype(out_ref.dtype)
        if step < chunks - 1:
            scale = spread(cols, base + 2 * heads, heads, head_dim)
            xs = (x.astype(jnp.float32) * scale).astype(jnp.bfloat16)
            fresh = jnp.dot(bt_ref[s, :, rows], xs, preferred_element_type=jnp.float32)
            at = s * chunks + c
            state = fresh if step == 0 else chunk_ref[at : at + 1] * state + fresh


def gate_kernel(head_dim, y_zero, y_one, z_ref, entry_ref, c_ref, in_ref, out_ref):
    strands, length, width = z_ref.shape
    y_refs = (y_zero, y_one)
    heads = width // head_dim
    for c in range(length // CHUNK):
        rows = slice(c * CHUNK, (c + 1) * CHUNK)
        total = 0.0
        for s in range(strands):
            carried = jnp.dot(c_ref[s, rows], in_ref[s], preferred_element_type=jnp.float32)
            y = y_refs[s][rows].astype(jnp.float32)
            y = y + carried * spread(entry_ref[0, rows], s * heads, heads, head_dim)
            total = total + y * silu(z_ref[s, rows].astype(jnp.float32))
        out_ref[rows] = total.astype(out_ref.dtype)


def neighbours(low_rows, high_rows):
    count = lax.axis_size("seq")
    forward = [(i, i + 1) for i in range(count - 1)]
    backward = [(i + 1, i) for i in range(count - 1)]
    return lax.ppermute(low_rows, "seq", forward), lax.ppermute(high_rows, "seq", backward)


def entering(local, states, across_work, line_work):
    count = lax.axis_size("seq")
    me = lax.axis_index("seq")
    half = local.shape[2] // 2
    core, across = me % 2, (me // 2) % 2
    row = lax.broadcasted_iota(jnp.int32, (1, local.shape[1], 1), 1)

    def decay(a):
        return a[..., states : states + 1, :].astype(jnp.float32)

    def joined(first, second, second_is_earlier):
        flag = second_is_earlier[:, None, None]
        a = jnp.where(flag, 1.0, decay(second))
        b = jnp.where(flag, decay(first), 1.0)
        first, second = first.astype(jnp.float32), second.astype(jnp.float32)
        both = jnp.where(row < states, a * first + b * second, first * second)
        return both.astype(jnp.bfloat16)

    def after(state, step, is_earlier):
        moved = decay(step) * state + step[..., :states, :].astype(jnp.float32)
        return jnp.where(is_earlier[:, None, None], moved, state)

    def mine(a):
        return lax.dynamic_slice_in_dim(a, core * half, half, a.ndim - 1)

    swap = [(i, i ^ 1) for i in range(count)]
    swap_pair = [(i, i ^ 2) for i in range(count)]
    up = [(i, i + 4) for i in range(count - 4)]
    down = [(i + 4, i) for i in range(count - 4)]

    other = lax.ppermute(local, "seq", swap)
    core_earlier = jnp.stack([core == 1, core == 0])
    chip = joined(mine(local), mine(other), core_earlier)
    chip_other = lax.ppermute(chip, "seq", swap_pair)
    results = []

    def beside(work, before, arrived):
        arrived, out = lax.optimization_barrier((arrived, work(before)))
        results.append(out)
        return arrived

    chip_other = beside(across_work, chip, chip_other)
    pair_earlier = jnp.stack([across == 1, across == 0])
    group = joined(chip, chip_other, pair_earlier)
    moving = [group[0], group[1]]
    total = [0.0, 0.0]
    factor = [1.0, 1.0]
    for step in range(count // 4 - 1):
        before = moving
        moving = [lax.ppermute(moving[0], "seq", up), lax.ppermute(moving[1], "seq", down)]
        if step < len(line_work):
            moving = beside(line_work[step], before, moving)
        for s in range(2):
            total[s] = total[s] + factor[s] * moving[s][:states].astype(jnp.float32)
            factor[s] = factor[s] * decay(moving[s])
    shape = (states, half)
    total = jnp.stack([jnp.broadcast_to(jnp.asarray(t, jnp.float32), shape) for t in total])
    chip_in = after(total, chip_other, pair_earlier).astype(jnp.bfloat16)
    rest = lax.ppermute(chip_in, "seq", swap)
    low = jnp.where(core == 0, chip_in, rest)
    high = jnp.where(core == 0, rest, chip_in)
    full = jnp.concatenate([low, high], axis=2).astype(jnp.float32)
    for work in line_work[max(count // 4 - 1, 0) :]:
        results.append(work(moving))
    return after(full, other, core_earlier).astype(jnp.bfloat16), results


def per_device(
    hidden, nucleotides, base_embed, x_proj, gate_proj, bc_proj, conv_x, bias_x, conv_bc,
    bias_bc, log_decay, d_skip, out_proj,
):
    taps, inner = conv_x.shape
    length = hidden.shape[1]
    head_count = d_skip.shape[0]
    head_dim = inner // head_count
    states = conv_bc.shape[1] // 2
    width = min(WIDTH, inner)
    blocks = inner // width
    heads = width // head_dim
    chunks = length // CHUNK
    inv_root = states ** (-0.5)

    r = jnp.arange(length)
    rates = log_decay.astype(jnp.float32)
    same = (r[:, None] // CHUNK) == (r[None, :] // CHUNK)
    older = [r[:, None] <= r[None, :], r[:, None] >= r[None, :]]

    def sums(masks):
        return jnp.stack(
            [
                jnp.dot(log_decay[s], masks[s].astype(jnp.bfloat16), preferred_element_type=jnp.float32)
                for s in range(2)
            ]
        )

    cum = sums([same & older[0], same & older[1]])
    left = sums([same & (r[:, None] > r[None, :]), same & (r[:, None] < r[None, :])])
    part = length // 2
    cum_all = sums(older)
    left_all = sums([r[:, None] > r[None, :], r[:, None] < r[None, :]])
    inject = jnp.sqrt(-jnp.expm1(2.0 * rates))
    tail_all = jnp.exp(left_all) * inject
    tail = jnp.exp(left) * inject
    entry = jnp.exp(cum) * inv_root
    row_terms = jnp.log2(inject * inv_root) - cum * LOG2E
    rows_arr = row_terms.reshape(2, blocks, heads, length).transpose(1, 0, 2, 3)
    rows_arr = rows_arr.reshape(blocks, 2 * heads, length)
    cols_arr = jnp.stack([cum * LOG2E, entry, tail], axis=1)
    cols_arr = cols_arr.reshape(2, 3, blocks, heads, length).transpose(2, 4, 0, 1, 3)
    cols_arr = cols_arr.reshape(blocks, length, 6 * heads)
    tail_arr = tail_all.reshape(2, blocks, heads, length).transpose(1, 3, 0, 2)
    tail_arr = tail_arr.reshape(blocks, length, 2 * heads)
    span_logs = jnp.sum(rates.reshape(2, head_count, chunks, CHUNK), axis=3)
    span_logs = jnp.repeat(span_logs.transpose(0, 2, 1), head_dim, axis=2)
    chunk_decay = jnp.exp(span_logs).reshape(2 * chunks, inner)
    shard_decay = jnp.exp(jnp.sum(span_logs, axis=1))
    entry_all = jnp.exp(cum_all) * inv_root
    entry_arr = entry_all.reshape(2, blocks, heads, length).transpose(1, 3, 0, 2)
    entry_arr = entry_arr.reshape(blocks, length, 2 * heads)
    skip = jnp.repeat(d_skip, head_dim)[None]

    inputs = jnp.concatenate(
        [
            strand_inputs(hidden[0], nucleotides, base_embed),
            strand_inputs(hidden[1], 3 - nucleotides, base_embed),
        ],
        axis=0,
    )
    inputs = lax.optimization_barrier(inputs)

    def project(weight):
        out = jnp.dot(inputs, weight, preferred_element_type=jnp.float32)
        return out.astype(jnp.bfloat16).reshape(2, length, -1)

    bc_pre = project(bc_proj)
    x_pre = project(x_proj)
    edge = taps - 1
    low = jnp.concatenate([x_pre[0, -edge:], bc_pre[0, -edge:]], axis=1)
    high = jnp.concatenate([x_pre[1, :edge], bc_pre[1, :edge]], axis=1)
    low, high = neighbours(low, high)
    x_rim = jnp.stack(
        [
            jnp.pad(low[:, :inner], ((8 - edge, 0), (0, 0))),
            jnp.pad(high[:, :inner], ((0, 8 - edge), (0, 0))),
        ]
    )
    bc_ext = [
        jnp.concatenate([low[:, inner:], bc_pre[0]], axis=0),
        jnp.concatenate([bc_pre[1], high[:, inner:]], axis=0),
    ]
    bc_conv = []
    for s in range(2):
        total = bias_bc
        for k in range(taps):
            at = k if s == 0 else edge - k
            total = total + conv_bc[k] * bc_ext[s][at : at + length].astype(jnp.float32)
        bc_conv.append(jax.nn.silu(total).astype(jnp.bfloat16))
    bc_conv = jnp.stack(bc_conv)
    c_rows = bc_conv[..., states:]
    b_cols = bc_conv[..., :states].transpose(0, 2, 1)

    params = pltpu.CompilerParams(dimension_semantics=("arbitrary",), vmem_limit_bytes=48 * 1024 * 1024)
    wide = pl.BlockSpec((2, length, width), lambda i: (0, 0, i))
    state_block = pl.BlockSpec((2, states, width), lambda i: (0, 0, i))
    whole = lambda a: pl.BlockSpec(a.shape, lambda i: (0,) * a.ndim)
    x_conv, local = pl.pallas_call(
        functools.partial(state_kernel, head_dim),
        grid=(blocks,),
        out_shape=(
            jax.ShapeDtypeStruct((2, length, inner), jnp.bfloat16),
            jax.ShapeDtypeStruct((2, states + PAD, inner), jnp.bfloat16),
        ),
        in_specs=[
            wide,
            pl.BlockSpec((2, 8, width), lambda i: (0, 0, i)),
            pl.BlockSpec((taps, width), lambda i: (0, i)),
            pl.BlockSpec((1, width), lambda i: (0, i)),
            pl.BlockSpec((1, length, 2 * heads), lambda i: (i, 0, 0)),
            pl.BlockSpec((2, width), lambda i: (0, i)),
            whole(b_cols),
        ],
        out_specs=(wide, pl.BlockSpec((2, states + PAD, width), lambda i: (0, 0, i))),
        scratch_shapes=[pltpu.VMEM((length + 16, width), jnp.float32)],
        compiler_params=params,
        name="conv_state",
    )(x_pre, x_rim, conv_x, bias_x[None], tail_arr, shard_decay, b_cols)

    def gate_rows(before):
        rows, _ = lax.optimization_barrier((inputs, before))
        out = jnp.dot(rows, gate_proj, preferred_element_type=jnp.float32)
        return out.astype(jnp.bfloat16).reshape(2, length, -1)

    def scan_strand(strand, before):
        x_in, _ = lax.optimization_barrier((x_conv, before))
        return pl.pallas_call(
        functools.partial(scan_kernel, head_dim, strand),
        grid=(blocks,),
        out_shape=jax.ShapeDtypeStruct((length, inner), jnp.bfloat16),
        in_specs=[
            pl.BlockSpec((1, length, width), lambda i: (strand, 0, i)),
            pl.BlockSpec((1, length, 6 * heads), lambda i: (i, 0, 0)),
            pl.BlockSpec((1, 2 * heads, length), lambda i: (i, 0, 0)),
            whole(b_cols),
            whole(c_rows),
            pl.BlockSpec((2 * chunks, width), lambda i: (0, i)),
            pl.BlockSpec((1, width), lambda i: (0, i)),
        ],
        out_specs=pl.BlockSpec((length, width), lambda i: (0, i)),
        scratch_shapes=[pltpu.VMEM((chunks, CHUNK, CHUNK), jnp.float32)],
        compiler_params=params,
        cost_estimate=pl.CostEstimate(
            flops=12 * length * inner * states, bytes_accessed=6 * length * inner, transcendentals=0
        ),
        name="scan",
    )(x_in, cols_arr, rows_arr, b_cols, c_rows, chunk_decay, skip)

    incoming, (z_pre, y_zero, y_one) = entering(
        local,
        states,
        gate_rows,
        [functools.partial(scan_strand, 0), functools.partial(scan_strand, 1)],
    )

    def scan_half(half, before=None):
        entered = incoming
        if before is not None:
            entered, _ = lax.optimization_barrier((incoming, before))
        rows_spec = pl.BlockSpec((2, part, width), lambda i: (0, half, i))
        return pl.pallas_call(
            functools.partial(gate_kernel, head_dim),
            grid=(blocks,),
            out_shape=jax.ShapeDtypeStruct((part, inner), jnp.bfloat16),
            in_specs=[
                pl.BlockSpec((part, width), lambda i: (half, i)),
                pl.BlockSpec((part, width), lambda i: (half, i)),
                rows_spec,
                pl.BlockSpec((1, part, 2 * heads), lambda i: (i, half, 0)),
                pl.BlockSpec((2, part, states), lambda i: (0, half, 0)),
                state_block,
            ],
            out_specs=pl.BlockSpec((part, width), lambda i: (0, i)),
            compiler_params=params,
            cost_estimate=pl.CostEstimate(
                flops=96 * part * inner * states, bytes_accessed=48 * part * inner, transcendentals=0
            ),
            name="gate",
        )(y_zero, y_one, z_pre, entry_arr, c_rows, entered)

    def out_part(weight, rows):
        return lax.dot_general(
            weight, rows, (((0,), (1,)), ((), ())), preferred_element_type=jnp.float32
        ).astype(jnp.bfloat16)

    if lax.axis_size("chan") == 2:
        size = out_proj.shape[1] // 2
        mine = lax.axis_index("chan")
        send_weight = lax.dynamic_slice_in_dim(out_proj, (1 - mine) * size, size, 1)
        own_weight = lax.dynamic_slice_in_dim(out_proj, mine * size, size, 1)
        first = scan_half(0)
        part_first = out_part(send_weight, first)
        sent_first = lax.ppermute(part_first, "chan", [(0, 1), (1, 0)])
        second = scan_half(1, part_first)
        sent_first, second = lax.optimization_barrier((sent_first, second))
        sent_second = lax.ppermute(out_part(send_weight, second), "chan", [(0, 1), (1, 0)])
        own = lax.optimization_barrier(out_part(own_weight, jnp.concatenate([first, second])))
        sent = jnp.concatenate([sent_first, sent_second], axis=1)
        return (own.astype(jnp.float32) + sent.astype(jnp.float32)).astype(jnp.bfloat16)
    mixed_in = jnp.concatenate([scan_half(0), scan_half(1)])
    return lax.psum_scatter(
        out_part(out_proj, mixed_in), "chan", scatter_dimension=0, tiled=True
    )


GROUP = 128
SUB = 64
HALO = 16
BLOCK = 256


def split_store(ref, s, rows, value, heads):
    high = value.astype(jnp.bfloat16)
    ref[s, rows, 0:heads] = high
    ref[s, rows, heads : 2 * heads] = (value - high.astype(jnp.float32)).astype(jnp.bfloat16)


def one_minus_exp(u):
    small = -u * (1 + u / 2 * (1 + u / 3 * (1 + u / 4 * (1 + u / 5 * (1 + u / 6)))))
    return jnp.where(u > -0.25, small, 1.0 - jnp.exp(u))


def nt(a, b):
    return lax.dot_general(a, b, (((1,), (1,)), ((), ())), preferred_element_type=jnp.float32)


def mm(a, b):
    return jnp.dot(a, b, preferred_element_type=jnp.float32)


def layer_kernel(
    head_dim, ids_ref, hid_ref, emb_ref, wx_hbm, wz_hbm, wbc_hbm, wo_hbm, tapx_ref, biasx_ref, tapbc_ref, biasbc_ref,
    ld_ref, skip_ref, out_ref,
    a_buf, w_buf, wz_buf, wbc_buf, ext_even, ext_odd, x_buf, xs_buf, st_buf, lh_buf, bt_buf, g_col, f_col, e_col, r_row,
    ids_low, ids_high, loc, core_in, chip, x_in, grp, grp_dec, z_out, z_in, ent_out, entry, gated, y_out, y_in, own,
    load_sem, wx_sem, halo_s, halo_r, core_s, core_r, x_s, x_r, z_s, z_r, ent_s, ent_r, y_s, y_r,
):
    _, length, depth = hid_ref.shape
    inner = wx_hbm.shape[1]
    feats = wo_hbm.shape[1] // 2
    taps = tapx_ref.shape[0]
    heads = inner // head_dim
    states = tapbc_ref.shape[1] // 2
    blocks = inner // BLOCK
    half = BLOCK // 2
    groups = length // GROUP
    subs = length // SUB
    inv_root = states ** (-0.5)
    bf, f32 = jnp.bfloat16, jnp.float32
    starts = (HALO, HALO + length)

    count = lax.axis_size("seq")
    me = lax.axis_index("seq")
    lane_mate = lax.axis_index("chan")
    core, across, line = me % 2, (me // 2) % 2, me // 4
    lines = count // 4
    right, left = (me + 1) % count, (me + count - 1) % count
    mate = me + 1 - 2 * core
    side = me + 2 - 4 * across
    up, down = (me + 4) % count, (me + count - 4) % count
    other_chan = 1 - lane_mate

    loads = [
        pltpu.make_async_copy(hid_ref.at[0], a_buf.at[pl.ds(starts[0], length)], load_sem.at[0]),
        pltpu.make_async_copy(hid_ref.at[1], a_buf.at[pl.ds(starts[1], length)], load_sem.at[1]),
        pltpu.make_async_copy(wbc_hbm, wbc_buf, load_sem.at[2]),
    ]

    def wx_load(j):
        cols = pl.ds(pl.multiple_of(j * BLOCK, BLOCK), BLOCK)
        return pltpu.make_async_copy(wx_hbm.at[:, cols], w_buf.at[:, cols], wx_sem.at[j])

    wz_load = pltpu.make_async_copy(wz_hbm, wz_buf, load_sem.at[3])
    wo_load = pltpu.make_async_copy(wo_hbm, w_buf, load_sem.at[4])
    for c in loads:
        c.start()
    for j in range(blocks):
        wx_load(j).start()
    wz_load.start()

    barrier = pltpu.get_barrier_semaphore()
    for peer in (right, left, mate, side, up, down):
        pl.semaphore_signal(barrier, inc=1, device_id={"seq": peer}, device_id_type=MESH)
    pl.semaphore_signal(barrier, inc=1, device_id={"chan": other_chan}, device_id_type=MESH)
    pl.semaphore_wait(barrier, 7)

    def send(src, dst, s_sem, r_sem, **where):
        return pltpu.make_async_remote_copy(
            src_ref=src, dst_ref=dst, send_sem=s_sem, recv_sem=r_sem, device_id=where, device_id_type=MESH
        )

    halos = [
        send(hid_ref.at[0, pl.ds(length - HALO, HALO)], a_buf.at[pl.ds(0, HALO)], halo_s.at[0], halo_r.at[0], seq=right),
        send(hid_ref.at[1, pl.ds(0, HALO)], a_buf.at[pl.ds(HALO + 2 * length, HALO)], halo_s.at[1], halo_r.at[1], seq=left),
        send(ids_ref, ids_low, halo_s.at[2], halo_r.at[2], seq=right),
        send(ids_ref, ids_high, halo_s.at[3], halo_r.at[3], seq=left),
    ]
    for c in halos:
        c.start()

    t = lax.broadcasted_iota(jnp.int32, (GROUP, GROUP), 0)
    r = lax.broadcasted_iota(jnp.int32, (GROUP, GROUP), 1)
    same = (t // SUB) == (r // SUB)
    low_half = (r % SUB) < (SUB // 2)
    older = (r <= t, r >= t)
    first_half = (low_half, jnp.logical_not(low_half))
    eye = (t == r).astype(f32)
    row = lax.broadcasted_iota(jnp.int32, (16, length), 0)
    pos = lax.broadcasted_iota(jnp.int32, (16, length), 1)
    row_id = lax.broadcasted_iota(jnp.int32, (16, heads), 0)
    in_low = ((pos % SUB) < (SUB // 2)).astype(f32)
    for s in range(2):
        q_mask = jnp.where(same, older[s].astype(f32) - first_half[s].astype(f32), 0.0)
        masks = jnp.concatenate([q_mask, older[s].astype(f32), eye], axis=0).astype(bf)
        before = jnp.zeros((1, heads), f32)
        for g in range(groups) if s == 0 else range(groups - 1, -1, -1):
            rows = slice(g * GROUP, (g + 1) * GROUP)
            res = nt(masks, ld_ref[s, :, rows])
            q, cum, rate = res[0:GROUP], res[GROUP : 2 * GROUP], res[2 * GROUP :]
            inject = jnp.sqrt(one_minus_exp(2.0 * rate))
            split_store(g_col, s, rows, jnp.exp(-q) * inject, heads)
            split_store(f_col, s, rows, jnp.exp(q) * inv_root, heads)
            cum = cum + before
            split_store(e_col, s, rows, jnp.exp(cum) * inv_root, heads)
            before = cum[GROUP - 1 :] if s == 0 else cum[0:1]
        first = in_low if s == 0 else 1.0 - in_low
        here = ((pos // SUB) == row).astype(f32)
        after = ((pos // SUB) == (row + 1 if s == 0 else row - 1)).astype(f32)
        pick = jnp.where(row < 8, here * (1.0 - first) + after * first, 1.0)
        logs = nt(pick.astype(bf), ld_ref[s])
        split_store(r_row, s, slice(0, 16), jnp.where(row_id == 9, skip_ref[...], jnp.exp(logs)), heads)

    code = lax.broadcasted_iota(jnp.int32, (8, GROUP), 0)
    table = jnp.concatenate([emb_ref[...].astype(f32), jnp.zeros((4, depth), f32)], axis=0).astype(bf)

    def looked(ids, flip):
        ids = 3 - ids if flip else ids
        n = ids.shape[1]
        hot = (code[:, :n] == jnp.broadcast_to(ids, (8, n))).astype(f32)
        return hot.T.astype(bf)

    for s in range(2):
        loads[s].wait()
        for g in range(groups):
            hot = looked(ids_ref[:, g * GROUP : (g + 1) * GROUP], s == 1)
            rows = slice(starts[s] + g * GROUP, starts[s] + (g + 1) * GROUP)
            a_buf[rows] = (a_buf[rows].astype(f32) + mm(hot, table)).astype(bf)
    for c in halos:
        c.wait()
    hot = looked(ids_low[:, length - GROUP :], False)[GROUP - HALO :]
    rows = slice(0, HALO)
    a_buf[rows] = jnp.where(me > 0, a_buf[rows].astype(f32) + mm(hot, table), 0.0).astype(bf)
    hot = looked(ids_high[:, :GROUP], True)[:HALO]
    rows = slice(HALO + 2 * length, 2 * HALO + 2 * length)
    a_buf[rows] = jnp.where(me < count - 1, a_buf[rows].astype(f32) + mm(hot, table), 0.0).astype(bf)

    def spread_rows(ext, value):
        for p in range(2):
            ext[p] = value[:, p * half : (p + 1) * half]

    def conv(ext, s, g, tap_rows, bias):
        parts = []
        for p in range(2):
            lanes = slice(p * half, (p + 1) * half)
            total = jnp.broadcast_to(bias[:, lanes], (GROUP, half))
            for k in range(taps):
                shift = k - (taps - 1) if s == 0 else (taps - 1) - k
                start = starts[s] + g * GROUP + shift
                total = total + tap_rows[k : k + 1, lanes] * ext[p, start : start + GROUP]
            parts.append(total + total * jnp.tanh(total))
        return jnp.concatenate(parts, axis=1)

    loads[2].wait()
    spread_rows(ext_odd, mm(a_buf[...], wbc_buf[...]))
    for s in range(2):
        keep = same & older[s]
        for g in range(groups):
            rows = slice(g * GROUP, (g + 1) * GROUP)
            both = conv(ext_odd, s, g, 0.5 * tapbc_ref[...], 0.5 * biasbc_ref[...])
            b, c = both[:, :states].astype(bf), both[:, states:].astype(bf)
            lh_buf[s, rows, 0:states] = c
            lh_buf[s, rows, states : states + GROUP] = jnp.where(keep, nt(c, b), 0.0).astype(bf)
            bt = b.astype(f32).T
            lower = r < SUB
            bt_buf[s, g, 0:states] = jnp.where(lower, bt, 0.0).astype(bf)
            bt_buf[s, g, states : 2 * states] = jnp.where(lower, 0.0, bt).astype(bf)

    head_row = lax.broadcasted_iota(jnp.int32, (2 * heads, BLOCK), 0) % heads
    head_lane = lax.broadcasted_iota(jnp.int32, (2 * heads, BLOCK), 1) // head_dim

    def spreader(j):
        return (head_row == head_lane + j * (BLOCK // head_dim)).astype(f32).astype(bf)

    def columns(j):
        return pl.ds(pl.multiple_of(j * BLOCK, BLOCK), BLOCK)

    def decay_of(a):
        return a[states : states + 1].astype(f32) + a[states + 1 : states + 2].astype(f32)

    def state_of(a):
        return a[0:states].astype(f32)

    def put(ref, at, s, state, decay):
        ref[at, s, 0:states] = state.astype(bf)
        high = decay.astype(bf)
        low = decay - high.astype(f32)
        pad_row = lax.broadcasted_iota(jnp.int32, (PAD, half), 0)
        ref[at, s, states : states + PAD] = jnp.where(pad_row == 0, high.astype(f32), low).astype(bf)

    def core_copy(b):
        return send(loc.at[b * 2 + 1 - core], core_in.at[b], core_s.at[b], core_r.at[b], seq=mate)

    def x_copy(b):
        return send(chip.at[b], x_in.at[b], x_s.at[b], x_r.at[b], seq=side)

    def z_copy(b, s):
        return send(z_out.at[b, s], z_in.at[b, s], z_s.at[b, s], z_r.at[b, s], seq=up if s == 0 else down)

    def ent_copy(b):
        span = pl.ds(pl.multiple_of(core * half, half), half)
        return send(ent_out.at[b], entry.at[b, :, :, span], ent_s.at[b], ent_r.at[b], seq=mate)

    def ent_arrived(b):
        span = pl.ds(pl.multiple_of((1 - core) * half, half), half)
        return send(ent_out.at[b], entry.at[b, :, :, span], ent_s.at[b], ent_r.at[b], seq=mate)

    def join(first, second, swapped):
        d1, d2 = decay_of(first), decay_of(second)
        s1, s2 = state_of(first), state_of(second)
        scale = jnp.where(swapped, d1, d2)
        state = jnp.where(swapped, scale * s2 + s1, scale * s1 + s2)
        return state, d1 * d2

    def chip_stage(b):
        core_copy(b).wait_recv()
        for s in range(2):
            mine, other = loc[b * 2 + core, s], core_in[b, s]
            swapped = (core == 1) if s == 0 else (core == 0)
            state, decay = join(mine, other, swapped)
            put(chip, b, s, state, decay)
        x_copy(b).start()

    def group_stage(b):
        x_copy(b).wait_recv()
        for s in range(2):
            swapped = (across == 1) if s == 0 else (across == 0)
            state, decay = join(chip[b, s], x_in[b, s], swapped)
            grp[b, s] = state
            grp_dec[b, s] = jnp.broadcast_to(decay, (8, half))
            z_out[b, s] = state.astype(bf)

            @pl.when(line == (0 if s == 0 else lines - 1))
            def _():
                z_copy(b, s).start()

    def line_stage(b, k):
        for s in range(2):
            at = k if s == 0 else lines - 1 - k

            @pl.when(line == at)
            def _():
                z_copy(b, s).wait_recv()
                if k < lines - 1:
                    state = grp_dec[b, s][0:1] * z_in[b, s].astype(f32) + grp[b, s]
                    z_out[b, s] = state.astype(bf)
                    z_copy(b, s).start()

    def enter_stage(b):
        for s in range(2):
            edge = line == (0 if s == 0 else lines - 1)
            entering = jnp.where(edge, 0.0, z_in[b, s].astype(f32))
            later_chip = (across == 1) if s == 0 else (across == 0)
            past = x_in[b, s]
            entering = jnp.where(later_chip, decay_of(past) * entering + state_of(past), entering)
            first = (core == 0) if s == 0 else (core == 1)
            mine, other = loc[b * 2 + core, s], core_in[b, s]
            dec = jnp.where(first, decay_of(mine), decay_of(other))
            adds = jnp.where(first, state_of(mine), state_of(other))
            second = dec * entering + adds
            span = pl.ds(pl.multiple_of(core * half, half), half)
            entry[b, s, :, span] = jnp.where(first, entering, second).astype(bf)
            ent_out[b, s] = jnp.where(first, second, entering).astype(bf)
        ent_copy(b).start()

    stages = [(2, chip_stage), (4, group_stage)]
    stages += [(4 + k, functools.partial(line_stage, k=k)) for k in range(1, lines)]
    stages += [(3 + lines, enter_stage)]

    def exchange(at):
        for lag, stage in stages:
            b = at - lag

            @pl.when((b >= 0) & (b < blocks))
            def _():
                stage(b)

    def project_x(j, ext):
        spread_rows(ext, mm(a_buf[...], w_buf[:, columns(j)]))

    def local_states(j, ext):
        cols = columns(j)
        spread_to = spreader(j)
        tap_rows, bias = 0.5 * tapx_ref[:, cols], 0.5 * biasx_ref[:, cols]
        for s in range(2):
            rows_at = mm(r_row[s], spread_to)
            state = None
            for g in range(groups) if s == 0 else range(groups - 1, -1, -1):
                rows = slice(g * GROUP, (g + 1) * GROUP)
                x = conv(ext, s, g, tap_rows, bias)
                x_buf[s, rows, cols] = x.astype(bf)
                xs = (x * mm(g_col[s, rows], spread_to)).astype(bf)
                xs_buf[s, rows, cols] = xs
                fresh = mm(bt_buf[s, g], xs)
                for p in (0, 1) if s == 0 else (1, 0):
                    c = 2 * g + p
                    part = fresh[p * states : (p + 1) * states]
                    if state is None:
                        st_buf[s, c, :, cols] = jnp.zeros((states, BLOCK), bf)
                        state = rows_at[c : c + 1] * part
                    else:
                        st_buf[s, c, :, cols] = state.astype(bf)
                        state = rows_at[c : c + 1] * (state + part)
            for p in range(2):
                lanes = slice(p * half, (p + 1) * half)
                put(loc, j * 2 + p, s, state[:, lanes], rows_at[8:9, lanes])
        core_copy(j).start()

    def two_blocks(i, _):
        j = 2 * i
        wx_load(j + 1).wait()
        exchange(j)
        project_x(j + 1, ext_odd)
        local_states(j, ext_even)
        wx_load(j + 2).wait()
        exchange(j + 1)
        project_x(j + 2, ext_even)
        local_states(j + 1, ext_odd)
        return 0

    wx_load(0).wait()
    project_x(0, ext_even)
    lax.fori_loop(0, blocks // 2 - 1, two_blocks, 0)
    wx_load(blocks - 1).wait()
    exchange(jnp.int32(blocks - 2))
    project_x(blocks - 1, ext_odd)
    local_states(blocks - 2, ext_even)
    wo_load.start()
    exchange(jnp.int32(blocks - 1))
    local_states(blocks - 1, ext_odd)

    def local_outputs(j, _):
        @pl.when((j == 0) | (j == 2) | (j == 5))
        def _():
            exchange(blocks + (j + 1) // 3)

        cols = columns(j)
        spread_to = spreader(j)
        for s in range(2):
            skip = mm(r_row[s], spread_to)[9:10]
            for g in range(groups):
                rows = slice(g * GROUP, (g + 1) * GROUP)
                factor = mm(f_col[s, rows], spread_to)
                xs = xs_buf[s, rows, cols]
                x = x_buf[s, rows, cols].astype(f32)
                ys = []
                for p in range(2):
                    c = 2 * g + p
                    rhs = jnp.concatenate([st_buf[s, c, :, cols], xs], axis=0)
                    ys.append(mm(lh_buf[s, c * SUB : (c + 1) * SUB], rhs))
                y = jnp.concatenate(ys, axis=0) * factor + skip * x
                x_buf[s, rows, cols] = y.astype(bf)
        return 0

    lax.fori_loop(0, blocks, local_outputs, 0)

    wz_load.wait()

    def gates(j, _):
        @pl.when((j == 0) | (j == 3) | (j == 6))
        def _():
            exchange(blocks + 3 + j // 3)

        cols = columns(j)
        h = 0.5 * mm(a_buf[HALO : HALO + 2 * length], wz_buf[:, cols])
        z = (h + h * jnp.tanh(h)).astype(bf)
        for s in range(2):
            xs_buf[s, :, cols] = z[s * length : (s + 1) * length]
        return 0

    lax.fori_loop(0, blocks, gates, 0)
    for at in range(blocks + 6, blocks + lines + 3):
        exchange(jnp.int32(at))
    for b in range(blocks):
        ent_arrived(b).wait_recv()
    wo_load.wait()

    def y_copy(i):
        return send(y_out.at[i], y_in.at[i], y_s.at[i], y_r.at[i], chan=other_chan)

    def rows_out(i, _):
        rows = pl.ds(pl.multiple_of(i * GROUP, GROUP), GROUP)

        def gate(j):
            cols = columns(j)
            spread_to = spreader(j)
            total = 0.0
            for s in range(2):
                carried = mm(lh_buf[s, rows, 0:states], entry[j, s])
                y = x_buf[s, rows, cols].astype(f32) + carried * mm(e_col[s, rows], spread_to)
                total = total + y * xs_buf[s, rows, cols].astype(f32)
            gated[:, cols] = total.astype(bf)

        def two_gates(n, _):
            gate(2 * n)
            gate(2 * n + 1)
            return 0

        lax.fori_loop(0, blocks // 2, two_gates, 0)

        def project(chan, target):
            cols = pl.ds(pl.multiple_of(chan * feats, BLOCK), feats)
            target[i] = mm(gated[...], w_buf[:, cols]).astype(bf)

        project(other_chan, y_out)
        y_copy(i).start()
        project(lane_mate, own)
        return 0

    lax.fori_loop(0, groups, rows_out, 0)

    for i in range(groups):
        y_copy(i).wait_recv()
        rows = slice(i * GROUP, (i + 1) * GROUP)
        out_ref[rows] = (own[i].astype(f32) + y_in[i].astype(f32)).astype(bf)

    for i in range(groups):
        y_copy(i).wait_send()
    for b in range(blocks):
        core_copy(b).wait_send()
        x_copy(b).wait_send()
        ent_copy(b).wait_send()

    @pl.when(line < lines - 1)
    def _():
        for b in range(blocks):
            z_copy(b, 0).wait_send()

    @pl.when(line > 0)
    def _():
        for b in range(blocks):
            z_copy(b, 1).wait_send()


def fused_device(
    hidden, nucleotides, base_embed, x_proj, gate_proj, bc_proj, conv_x, bias_x, conv_bc,
    bias_bc, log_decay, d_skip, out_proj,
):
    length, depth = hidden.shape[1:]
    inner = x_proj.shape[1]
    feats = out_proj.shape[1] // 2
    heads = d_skip.shape[0]
    states = conv_bc.shape[1] // 2
    blocks, groups, subs, half = inner // BLOCK, length // GROUP, length // SUB, BLOCK // 2
    rows = 2 * length + 2 * HALO
    bf, f32 = jnp.bfloat16, jnp.float32
    vmem, dma = pltpu.VMEM, pltpu.SemaphoreType.DMA
    small = pl.BlockSpec(memory_space=pltpu.VMEM)
    large = pl.BlockSpec(memory_space=pl.ANY)
    pair = (blocks, 2, states + PAD, half)
    out = pl.pallas_call(
        functools.partial(layer_kernel, inner // heads),
        out_shape=jax.ShapeDtypeStruct((length, feats), bf),
        in_specs=[small, large, small, large, large, large, large] + [small] * 6,
        out_specs=small,
        scratch_shapes=[
            vmem((rows, depth), bf),
            vmem((depth, inner), bf),
            vmem((depth, inner), bf),
            vmem((depth, 2 * states), bf),
            vmem((2, rows, BLOCK // 2), f32),
            vmem((2, rows, BLOCK // 2), f32),
            vmem((2, length, inner), bf),
            vmem((2, length, inner), bf),
            vmem((2, subs, states, inner), bf),
            vmem((2, length, states + GROUP), bf),
            vmem((2, groups, 2 * states, GROUP), bf),
            vmem((2, length, 2 * heads), bf),
            vmem((2, length, 2 * heads), bf),
            vmem((2, length, 2 * heads), bf),
            vmem((2, 16, 2 * heads), bf),
            vmem((1, length), jnp.int32),
            vmem((1, length), jnp.int32),
            vmem((2 * blocks, 2, states + PAD, half), bf),
            vmem(pair, bf),
            vmem(pair, bf),
            vmem(pair, bf),
            vmem((blocks, 2, states, half), f32),
            vmem((blocks, 2, 8, half), f32),
            vmem((blocks, 2, states, half), bf),
            vmem((blocks, 2, states, half), bf),
            vmem((blocks, 2, states, half), bf),
            vmem((blocks, 2, states, BLOCK), bf),
            vmem((GROUP, inner), bf),
            vmem((groups, GROUP, feats), bf),
            vmem((groups, GROUP, feats), bf),
            vmem((groups, GROUP, feats), bf),
            dma((5,)), dma((blocks,)), dma((4,)), dma((4,)),
            dma((blocks,)), dma((blocks,)), dma((blocks,)), dma((blocks,)),
            dma((blocks, 2)), dma((blocks, 2)), dma((blocks,)), dma((blocks,)),
            dma((groups,)), dma((groups,)),
        ],
        compiler_params=pltpu.CompilerParams(
            collective_id=0, has_side_effects=True, vmem_limit_bytes=67043328
        ),
        name="layer",
    )(
        nucleotides[None], hidden, base_embed, x_proj, gate_proj, bc_proj, out_proj, conv_x, bias_x[None], conv_bc,
        bias_bc[None], log_decay, d_skip[None],
    )
    return out.T


def any_device(*args):
    hidden, x_proj, conv_bc = args[0], args[3], args[8]
    fits = lax.axis_size("chan") == 2 and lax.axis_size("seq") % 4 == 0 and lax.axis_size("seq") >= 8
    fits = fits and hidden.shape[1] == 8 * SUB and conv_bc.shape[1] == BLOCK
    fits = fits and x_proj.shape[1] % (2 * BLOCK) == 0 and x_proj.shape[1] >= 8 * BLOCK
    return fused_device(*args) if fits else per_device(*args)


def solution(mesh):
    in_specs = (
        P(None, "seq", None), P("seq"), P(), P(None, "chan"), P(None, "chan"), P(),
        P(None, "chan"), P("chan"), P(), P(), P(None, "chan", "seq"), P("chan"), P("chan", None),
    )
    return jax.shard_map(
        any_device, mesh=mesh, in_specs=in_specs, out_specs=P("chan", "seq"), check_vma=False
    )
```

```python
import functools

import jax
import jax.numpy as jnp
from jax import lax
from jax.experimental import pallas as pl
from jax.experimental.pallas import tpu as pltpu
from jax.sharding import PartitionSpec as P

CHUNK = 128
WIDTH = 256
PAD = 16
LOG2E = 1.4426950408889634
MESH = pl.DeviceIdType.MESH


def silu(v):
    return v * (0.5 + 0.5 * jnp.tanh(0.5 * v))


def strand_inputs(hidden_rows, ids, base_embed):
    table = base_embed.astype(jnp.float32)
    pick = ids[:, None]
    low = jnp.where(pick == 0, table[0], table[1])
    high = jnp.where(pick == 2, table[2], table[3])
    looked = jnp.where(pick < 2, low, high)
    return (hidden_rows.astype(jnp.float32) + looked).astype(jnp.bfloat16)


def spread(cols, first, heads, head_dim):
    rows = cols.shape[0]
    per = 128 // head_dim
    lane = lax.broadcasted_iota(jnp.int32, (rows, 128), 1)
    tiles = []
    for t in range(heads // per):
        tile = jnp.broadcast_to(cols[:, first + t * per : first + t * per + 1], (rows, 128))
        for p in range(1, per):
            h = first + t * per + p
            tile = jnp.where(
                lane >= p * head_dim, jnp.broadcast_to(cols[:, h : h + 1], (rows, 128)), tile
            )
        tiles.append(tile)
    return jnp.concatenate(tiles, axis=1)


def state_kernel(head_dim, x_ref, rim_ref, taps_ref, bias_ref, tail_ref, decay_ref, bt_ref, conv_ref, state_ref, ext):
    strands, length, width = x_ref.shape
    taps = taps_ref.shape[0]
    heads = width // head_dim
    for s in range(strands):
        ext[8 : 8 + length] = x_ref[s].astype(jnp.float32)
        if s == 0:
            ext[0:8] = rim_ref[s].astype(jnp.float32)
        else:
            ext[8 + length : 16 + length] = rim_ref[s].astype(jnp.float32)
        chunks = length // CHUNK
        for step in range(chunks):
            c = step if s == 0 else chunks - 1 - step
            total = jnp.broadcast_to(bias_ref[...], (CHUNK, width))
            for k in range(taps):
                shift = k - (taps - 1) if s == 0 else (taps - 1) - k
                start = 8 + c * CHUNK + shift
                total = total + taps_ref[k : k + 1] * ext[start : start + CHUNK]
            rows = slice(c * CHUNK, (c + 1) * CHUNK)
            x = silu(total).astype(jnp.bfloat16)
            conv_ref[s, rows] = x
            scale = spread(tail_ref[0, rows], s * heads, heads, head_dim)
            xs = (x.astype(jnp.float32) * scale).astype(jnp.bfloat16)
            part = jnp.dot(bt_ref[s, :, rows], xs, preferred_element_type=jnp.float32)
            if step == 0:
                acc = part
            else:
                acc = acc + part
        states = acc.shape[0]
        state_ref[s, :states] = acc.astype(state_ref.dtype)
        state_ref[s, states:] = jnp.broadcast_to(
            decay_ref[s : s + 1], (PAD, width)
        ).astype(state_ref.dtype)


def scan_kernel(head_dim, s, x_ref, cols_ref, rows_ref, bt_ref, c_ref, chunk_ref, skip_ref, out_ref, scores):
    _, length, width = x_ref.shape
    heads = width // head_dim
    per = 128 // head_dim
    chunks = length // CHUNK

    @pl.when(pl.program_id(0) == 0)
    def _():
        t = lax.broadcasted_iota(jnp.int32, (CHUNK, CHUNK), 0)
        r = lax.broadcasted_iota(jnp.int32, (CHUNK, CHUNK), 1)
        keep = (r <= t) if s == 0 else (r >= t)
        for c in range(chunks):
            rows = slice(c * CHUNK, (c + 1) * CHUNK)
            sc = jnp.dot(c_ref[s, rows], bt_ref[s, :, rows], preferred_element_type=jnp.float32)
            scores[c] = jnp.where(keep, sc, 0.0)

    lane = lax.broadcasted_iota(jnp.int32, (CHUNK, 128), 1)
    state = None
    order = range(chunks) if s == 0 else range(chunks - 1, -1, -1)
    for step, c in enumerate(order):
        rows = slice(c * CHUNK, (c + 1) * CHUNK)
        cols = cols_ref[0, rows]
        base = s * 3 * heads
        x = x_ref[0, rows]
        sc = scores[c]
        y = skip_ref[...] * x.astype(jnp.float32)
        if step > 0:
            carried = jnp.dot(
                c_ref[s, rows], state.astype(jnp.bfloat16), preferred_element_type=jnp.float32
            )
            y = y + carried * spread(cols, base + heads, heads, head_dim)
        tiles = []
        for t in range(heads // per):
            xt = x[:, t * 128 : (t + 1) * 128]
            lhs, rhs = [], []
            for p in range(per):
                h = t * per + p
                gap = cols[:, base + h : base + h + 1] + rows_ref[0, s * heads + h : s * heads + h + 1, rows]
                lhs.append((sc * jnp.exp2(jnp.minimum(gap, 0.0))).astype(jnp.bfloat16))
                inside = (lane >= p * head_dim) & (lane < (p + 1) * head_dim)
                rhs.append(jnp.where(inside, xt, jnp.zeros_like(xt)))
            tiles.append(
                jnp.dot(
                    jnp.concatenate(lhs, axis=1),
                    jnp.concatenate(rhs, axis=0),
                    preferred_element_type=jnp.float32,
                )
            )
        y = y + jnp.concatenate(tiles, axis=1)
        out_ref[rows] = y.astype(out_ref.dtype)
        if step < chunks - 1:
            scale = spread(cols, base + 2 * heads, heads, head_dim)
            xs = (x.astype(jnp.float32) * scale).astype(jnp.bfloat16)
            fresh = jnp.dot(bt_ref[s, :, rows], xs, preferred_element_type=jnp.float32)
            at = s * chunks + c
            state = fresh if step == 0 else chunk_ref[at : at + 1] * state + fresh


def gate_kernel(head_dim, y_zero, y_one, z_ref, entry_ref, c_ref, in_ref, out_ref):
    strands, length, width = z_ref.shape
    y_refs = (y_zero, y_one)
    heads = width // head_dim
    for c in range(length // CHUNK):
        rows = slice(c * CHUNK, (c + 1) * CHUNK)
        total = 0.0
        for s in range(strands):
            carried = jnp.dot(c_ref[s, rows], in_ref[s], preferred_element_type=jnp.float32)
            y = y_refs[s][rows].astype(jnp.float32)
            y = y + carried * spread(entry_ref[0, rows], s * heads, heads, head_dim)
            total = total + y * silu(z_ref[s, rows].astype(jnp.float32))
        out_ref[rows] = total.astype(out_ref.dtype)


def neighbours(low_rows, high_rows):
    count = lax.axis_size("seq")
    forward = [(i, i + 1) for i in range(count - 1)]
    backward = [(i + 1, i) for i in range(count - 1)]
    return lax.ppermute(low_rows, "seq", forward), lax.ppermute(high_rows, "seq", backward)


def entering(local, states, across_work, line_work):
    count = lax.axis_size("seq")
    me = lax.axis_index("seq")
    half = local.shape[2] // 2
    core, across = me % 2, (me // 2) % 2
    row = lax.broadcasted_iota(jnp.int32, (1, local.shape[1], 1), 1)

    def decay(a):
        return a[..., states : states + 1, :].astype(jnp.float32)

    def joined(first, second, second_is_earlier):
        flag = second_is_earlier[:, None, None]
        a = jnp.where(flag, 1.0, decay(second))
        b = jnp.where(flag, decay(first), 1.0)
        first, second = first.astype(jnp.float32), second.astype(jnp.float32)
        both = jnp.where(row < states, a * first + b * second, first * second)
        return both.astype(jnp.bfloat16)

    def after(state, step, is_earlier):
        moved = decay(step) * state + step[..., :states, :].astype(jnp.float32)
        return jnp.where(is_earlier[:, None, None], moved, state)

    def mine(a):
        return lax.dynamic_slice_in_dim(a, core * half, half, a.ndim - 1)

    swap = [(i, i ^ 1) for i in range(count)]
    swap_pair = [(i, i ^ 2) for i in range(count)]
    up = [(i, i + 4) for i in range(count - 4)]
    down = [(i + 4, i) for i in range(count - 4)]

    other = lax.ppermute(local, "seq", swap)
    core_earlier = jnp.stack([core == 1, core == 0])
    chip = joined(mine(local), mine(other), core_earlier)
    chip_other = lax.ppermute(chip, "seq", swap_pair)
    results = []

    def beside(work, before, arrived):
        arrived, out = lax.optimization_barrier((arrived, work(before)))
        results.append(out)
        return arrived

    chip_other = beside(across_work, chip, chip_other)
    pair_earlier = jnp.stack([across == 1, across == 0])
    group = joined(chip, chip_other, pair_earlier)
    moving = [group[0], group[1]]
    total = [0.0, 0.0]
    factor = [1.0, 1.0]
    for step in range(count // 4 - 1):
        before = moving
        moving = [lax.ppermute(moving[0], "seq", up), lax.ppermute(moving[1], "seq", down)]
        if step < len(line_work):
            moving = beside(line_work[step], before, moving)
        for s in range(2):
            total[s] = total[s] + factor[s] * moving[s][:states].astype(jnp.float32)
            factor[s] = factor[s] * decay(moving[s])
    shape = (states, half)
    total = jnp.stack([jnp.broadcast_to(jnp.asarray(t, jnp.float32), shape) for t in total])
    chip_in = after(total, chip_other, pair_earlier).astype(jnp.bfloat16)
    rest = lax.ppermute(chip_in, "seq", swap)
    low = jnp.where(core == 0, chip_in, rest)
    high = jnp.where(core == 0, rest, chip_in)
    full = jnp.concatenate([low, high], axis=2).astype(jnp.float32)
    for work in line_work[max(count // 4 - 1, 0) :]:
        results.append(work(moving))
    return after(full, other, core_earlier).astype(jnp.bfloat16), results


def per_device(
    hidden, nucleotides, base_embed, x_proj, gate_proj, bc_proj, conv_x, bias_x, conv_bc,
    bias_bc, log_decay, d_skip, out_proj,
):
    taps, inner = conv_x.shape
    length = hidden.shape[1]
    head_count = d_skip.shape[0]
    head_dim = inner // head_count
    states = conv_bc.shape[1] // 2
    width = min(WIDTH, inner)
    blocks = inner // width
    heads = width // head_dim
    chunks = length // CHUNK
    inv_root = states ** (-0.5)

    r = jnp.arange(length)
    rates = log_decay.astype(jnp.float32)
    same = (r[:, None] // CHUNK) == (r[None, :] // CHUNK)
    older = [r[:, None] <= r[None, :], r[:, None] >= r[None, :]]

    def sums(masks):
        return jnp.stack(
            [
                jnp.dot(log_decay[s], masks[s].astype(jnp.bfloat16), preferred_element_type=jnp.float32)
                for s in range(2)
            ]
        )

    cum = sums([same & older[0], same & older[1]])
    left = sums([same & (r[:, None] > r[None, :]), same & (r[:, None] < r[None, :])])
    part = length // 2
    cum_all = sums(older)
    left_all = sums([r[:, None] > r[None, :], r[:, None] < r[None, :]])
    inject = jnp.sqrt(-jnp.expm1(2.0 * rates))
    tail_all = jnp.exp(left_all) * inject
    tail = jnp.exp(left) * inject
    entry = jnp.exp(cum) * inv_root
    row_terms = jnp.log2(inject * inv_root) - cum * LOG2E
    rows_arr = row_terms.reshape(2, blocks, heads, length).transpose(1, 0, 2, 3)
    rows_arr = rows_arr.reshape(blocks, 2 * heads, length)
    cols_arr = jnp.stack([cum * LOG2E, entry, tail], axis=1)
    cols_arr = cols_arr.reshape(2, 3, blocks, heads, length).transpose(2, 4, 0, 1, 3)
    cols_arr = cols_arr.reshape(blocks, length, 6 * heads)
    tail_arr = tail_all.reshape(2, blocks, heads, length).transpose(1, 3, 0, 2)
    tail_arr = tail_arr.reshape(blocks, length, 2 * heads)
    span_logs = jnp.sum(rates.reshape(2, head_count, chunks, CHUNK), axis=3)
    span_logs = jnp.repeat(span_logs.transpose(0, 2, 1), head_dim, axis=2)
    chunk_decay = jnp.exp(span_logs).reshape(2 * chunks, inner)
    shard_decay = jnp.exp(jnp.sum(span_logs, axis=1))
    entry_all = jnp.exp(cum_all) * inv_root
    entry_arr = entry_all.reshape(2, blocks, heads, length).transpose(1, 3, 0, 2)
    entry_arr = entry_arr.reshape(blocks, length, 2 * heads)
    skip = jnp.repeat(d_skip, head_dim)[None]

    inputs = jnp.concatenate(
        [
            strand_inputs(hidden[0], nucleotides, base_embed),
            strand_inputs(hidden[1], 3 - nucleotides, base_embed),
        ],
        axis=0,
    )
    inputs = lax.optimization_barrier(inputs)

    def project(weight):
        out = jnp.dot(inputs, weight, preferred_element_type=jnp.float32)
        return out.astype(jnp.bfloat16).reshape(2, length, -1)

    bc_pre = project(bc_proj)
    x_pre = project(x_proj)
    edge = taps - 1
    low = jnp.concatenate([x_pre[0, -edge:], bc_pre[0, -edge:]], axis=1)
    high = jnp.concatenate([x_pre[1, :edge], bc_pre[1, :edge]], axis=1)
    low, high = neighbours(low, high)
    x_rim = jnp.stack(
        [
            jnp.pad(low[:, :inner], ((8 - edge, 0), (0, 0))),
            jnp.pad(high[:, :inner], ((0, 8 - edge), (0, 0))),
        ]
    )
    bc_ext = [
        jnp.concatenate([low[:, inner:], bc_pre[0]], axis=0),
        jnp.concatenate([bc_pre[1], high[:, inner:]], axis=0),
    ]
    bc_conv = []
    for s in range(2):
        total = bias_bc
        for k in range(taps):
            at = k if s == 0 else edge - k
            total = total + conv_bc[k] * bc_ext[s][at : at + length].astype(jnp.float32)
        bc_conv.append(jax.nn.silu(total).astype(jnp.bfloat16))
    bc_conv = jnp.stack(bc_conv)
    c_rows = bc_conv[..., states:]
    b_cols = bc_conv[..., :states].transpose(0, 2, 1)

    params = pltpu.CompilerParams(dimension_semantics=("arbitrary",), vmem_limit_bytes=48 * 1024 * 1024)
    wide = pl.BlockSpec((2, length, width), lambda i: (0, 0, i))
    state_block = pl.BlockSpec((2, states, width), lambda i: (0, 0, i))
    whole = lambda a: pl.BlockSpec(a.shape, lambda i: (0,) * a.ndim)
    x_conv, local = pl.pallas_call(
        functools.partial(state_kernel, head_dim),
        grid=(blocks,),
        out_shape=(
            jax.ShapeDtypeStruct((2, length, inner), jnp.bfloat16),
            jax.ShapeDtypeStruct((2, states + PAD, inner), jnp.bfloat16),
        ),
        in_specs=[
            wide,
            pl.BlockSpec((2, 8, width), lambda i: (0, 0, i)),
            pl.BlockSpec((taps, width), lambda i: (0, i)),
            pl.BlockSpec((1, width), lambda i: (0, i)),
            pl.BlockSpec((1, length, 2 * heads), lambda i: (i, 0, 0)),
            pl.BlockSpec((2, width), lambda i: (0, i)),
            whole(b_cols),
        ],
        out_specs=(wide, pl.BlockSpec((2, states + PAD, width), lambda i: (0, 0, i))),
        scratch_shapes=[pltpu.VMEM((length + 16, width), jnp.float32)],
        compiler_params=params,
        name="conv_state",
    )(x_pre, x_rim, conv_x, bias_x[None], tail_arr, shard_decay, b_cols)

    def gate_rows(before):
        rows, _ = lax.optimization_barrier((inputs, before))
        out = jnp.dot(rows, gate_proj, preferred_element_type=jnp.float32)
        return out.astype(jnp.bfloat16).reshape(2, length, -1)

    def scan_strand(strand, before):
        x_in, _ = lax.optimization_barrier((x_conv, before))
        return pl.pallas_call(
        functools.partial(scan_kernel, head_dim, strand),
        grid=(blocks,),
        out_shape=jax.ShapeDtypeStruct((length, inner), jnp.bfloat16),
        in_specs=[
            pl.BlockSpec((1, length, width), lambda i: (strand, 0, i)),
            pl.BlockSpec((1, length, 6 * heads), lambda i: (i, 0, 0)),
            pl.BlockSpec((1, 2 * heads, length), lambda i: (i, 0, 0)),
            whole(b_cols),
            whole(c_rows),
            pl.BlockSpec((2 * chunks, width), lambda i: (0, i)),
            pl.BlockSpec((1, width), lambda i: (0, i)),
        ],
        out_specs=pl.BlockSpec((length, width), lambda i: (0, i)),
        scratch_shapes=[pltpu.VMEM((chunks, CHUNK, CHUNK), jnp.float32)],
        compiler_params=params,
        cost_estimate=pl.CostEstimate(
            flops=12 * length * inner * states, bytes_accessed=6 * length * inner, transcendentals=0
        ),
        name="scan",
    )(x_in, cols_arr, rows_arr, b_cols, c_rows, chunk_decay, skip)

    incoming, (z_pre, y_zero, y_one) = entering(
        local,
        states,
        gate_rows,
        [functools.partial(scan_strand, 0), functools.partial(scan_strand, 1)],
    )

    def scan_half(half, before=None):
        entered = incoming
        if before is not None:
            entered, _ = lax.optimization_barrier((incoming, before))
        rows_spec = pl.BlockSpec((2, part, width), lambda i: (0, half, i))
        return pl.pallas_call(
            functools.partial(gate_kernel, head_dim),
            grid=(blocks,),
            out_shape=jax.ShapeDtypeStruct((part, inner), jnp.bfloat16),
            in_specs=[
                pl.BlockSpec((part, width), lambda i: (half, i)),
                pl.BlockSpec((part, width), lambda i: (half, i)),
                rows_spec,
                pl.BlockSpec((1, part, 2 * heads), lambda i: (i, half, 0)),
                pl.BlockSpec((2, part, states), lambda i: (0, half, 0)),
                state_block,
            ],
            out_specs=pl.BlockSpec((part, width), lambda i: (0, i)),
            compiler_params=params,
            cost_estimate=pl.CostEstimate(
                flops=96 * part * inner * states, bytes_accessed=48 * part * inner, transcendentals=0
            ),
            name="gate",
        )(y_zero, y_one, z_pre, entry_arr, c_rows, entered)

    def out_part(weight, rows):
        return lax.dot_general(
            weight, rows, (((0,), (1,)), ((), ())), preferred_element_type=jnp.float32
        ).astype(jnp.bfloat16)

    if lax.axis_size("chan") == 2:
        size = out_proj.shape[1] // 2
        mine = lax.axis_index("chan")
        send_weight = lax.dynamic_slice_in_dim(out_proj, (1 - mine) * size, size, 1)
        own_weight = lax.dynamic_slice_in_dim(out_proj, mine * size, size, 1)
        first = scan_half(0)
        part_first = out_part(send_weight, first)
        sent_first = lax.ppermute(part_first, "chan", [(0, 1), (1, 0)])
        second = scan_half(1, part_first)
        sent_first, second = lax.optimization_barrier((sent_first, second))
        sent_second = lax.ppermute(out_part(send_weight, second), "chan", [(0, 1), (1, 0)])
        own = lax.optimization_barrier(out_part(own_weight, jnp.concatenate([first, second])))
        sent = jnp.concatenate([sent_first, sent_second], axis=1)
        return (own.astype(jnp.float32) + sent.astype(jnp.float32)).astype(jnp.bfloat16)
    mixed_in = jnp.concatenate([scan_half(0), scan_half(1)])
    return lax.psum_scatter(
        out_part(out_proj, mixed_in), "chan", scatter_dimension=0, tiled=True
    )


GROUP = 128
SUB = 64
HALO = 16
BLOCK = 256


def split_store(ref, s, rows, value, heads):
    high = value.astype(jnp.bfloat16)
    ref[s, rows, 0:heads] = high
    ref[s, rows, heads : 2 * heads] = (value - high.astype(jnp.float32)).astype(jnp.bfloat16)


def one_minus_exp(u):
    small = -u * (1 + u / 2 * (1 + u / 3 * (1 + u / 4 * (1 + u / 5 * (1 + u / 6)))))
    return jnp.where(u > -0.25, small, 1.0 - jnp.exp(u))


def nt(a, b):
    return lax.dot_general(a, b, (((1,), (1,)), ((), ())), preferred_element_type=jnp.float32)


def mm(a, b):
    return jnp.dot(a, b, preferred_element_type=jnp.float32)


def layer_kernel(
    head_dim, ids_ref, hid_ref, emb_ref, wx_hbm, wz_hbm, wbc_hbm, wo_hbm, tapx_ref, biasx_ref, tapbc_ref, biasbc_ref,
    ld_ref, skip_ref, out_ref,
    a_buf, w_buf, wz_buf, wbc_buf, ext_even, ext_odd, x_buf, xs_buf, st_buf, lh_buf, bt_buf, g_col, f_col, e_col, r_row,
    ids_low, ids_high, loc, core_in, chip, x_in, grp, grp_dec, z_out, z_in, ent_out, entry, gated, y_out, y_in, own,
    load_sem, wx_sem, halo_s, halo_r, core_s, core_r, x_s, x_r, z_s, z_r, ent_s, ent_r, y_s, y_r,
):
    _, length, depth = hid_ref.shape
    inner = wx_hbm.shape[1]
    feats = wo_hbm.shape[1] // 2
    taps = tapx_ref.shape[0]
    heads = inner // head_dim
    states = tapbc_ref.shape[1] // 2
    blocks = inner // BLOCK
    half = BLOCK // 2
    groups = length // GROUP
    subs = length // SUB
    inv_root = states ** (-0.5)
    bf, f32 = jnp.bfloat16, jnp.float32
    starts = (HALO, HALO + length)

    count = lax.axis_size("seq")
    me = lax.axis_index("seq")
    lane_mate = lax.axis_index("chan")
    core, across, line = me % 2, (me // 2) % 2, me // 4
    lines = count // 4
    right, left = (me + 1) % count, (me + count - 1) % count
    mate = me + 1 - 2 * core
    side = me + 2 - 4 * across
    up, down = (me + 4) % count, (me + count - 4) % count
    other_chan = 1 - lane_mate

    loads = [
        pltpu.make_async_copy(hid_ref.at[0], a_buf.at[pl.ds(starts[0], length)], load_sem.at[0]),
        pltpu.make_async_copy(hid_ref.at[1], a_buf.at[pl.ds(starts[1], length)], load_sem.at[1]),
        pltpu.make_async_copy(wbc_hbm, wbc_buf, load_sem.at[2]),
    ]

    def wx_load(j):
        cols = pl.ds(pl.multiple_of(j * BLOCK, BLOCK), BLOCK)
        return pltpu.make_async_copy(wx_hbm.at[:, cols], w_buf.at[:, cols], wx_sem.at[j])

    wz_load = pltpu.make_async_copy(wz_hbm, wz_buf, load_sem.at[3])
    wo_load = pltpu.make_async_copy(wo_hbm, w_buf, load_sem.at[4])
    for c in loads:
        c.start()

    barrier = pltpu.get_barrier_semaphore()
    for peer in (right, left, mate, side, up, down):
        pl.semaphore_signal(barrier, inc=1, device_id={"seq": peer}, device_id_type=MESH)
    pl.semaphore_signal(barrier, inc=1, device_id={"chan": other_chan}, device_id_type=MESH)
    def send(src, dst, s_sem, r_sem, **where):
        return pltpu.make_async_remote_copy(
            src_ref=src, dst_ref=dst, send_sem=s_sem, recv_sem=r_sem, device_id=where, device_id_type=MESH
        )

    halos = [
        send(hid_ref.at[0, pl.ds(length - HALO, HALO)], a_buf.at[pl.ds(0, HALO)], halo_s.at[0], halo_r.at[0], seq=right),
        send(hid_ref.at[1, pl.ds(0, HALO)], a_buf.at[pl.ds(HALO + 2 * length, HALO)], halo_s.at[1], halo_r.at[1], seq=left),
        send(ids_ref, ids_low, halo_s.at[2], halo_r.at[2], seq=right),
        send(ids_ref, ids_high, halo_s.at[3], halo_r.at[3], seq=left),
    ]

    t = lax.broadcasted_iota(jnp.int32, (GROUP, GROUP), 0)
    r = lax.broadcasted_iota(jnp.int32, (GROUP, GROUP), 1)
    same = (t // SUB) == (r // SUB)
    low_half = (r % SUB) < (SUB // 2)
    older = (r <= t, r >= t)
    first_half = (low_half, jnp.logical_not(low_half))
    eye = (t == r).astype(f32)
    row = lax.broadcasted_iota(jnp.int32, (16, length), 0)
    pos = lax.broadcasted_iota(jnp.int32, (16, length), 1)
    row_id = lax.broadcasted_iota(jnp.int32, (16, heads), 0)
    in_low = ((pos % SUB) < (SUB // 2)).astype(f32)
    for s in range(2):
        q_mask = jnp.where(same, older[s].astype(f32) - first_half[s].astype(f32), 0.0)
        masks = jnp.concatenate([q_mask, older[s].astype(f32), eye], axis=0).astype(bf)
        before = jnp.zeros((1, heads), f32)
        for g in range(groups) if s == 0 else range(groups - 1, -1, -1):
            rows = slice(g * GROUP, (g + 1) * GROUP)
            res = nt(masks, ld_ref[s, :, rows])
            q, cum, rate = res[0:GROUP], res[GROUP : 2 * GROUP], res[2 * GROUP :]
            inject = jnp.sqrt(one_minus_exp(2.0 * rate))
            split_store(g_col, s, rows, jnp.exp(-q) * inject, heads)
            split_store(f_col, s, rows, jnp.exp(q) * inv_root, heads)
            cum = cum + before
            split_store(e_col, s, rows, jnp.exp(cum) * inv_root, heads)
            before = cum[GROUP - 1 :] if s == 0 else cum[0:1]
        first = in_low if s == 0 else 1.0 - in_low
        here = ((pos // SUB) == row).astype(f32)
        after = ((pos // SUB) == (row + 1 if s == 0 else row - 1)).astype(f32)
        pick = jnp.where(row < 8, here * (1.0 - first) + after * first, 1.0)
        logs = nt(pick.astype(bf), ld_ref[s])
        split_store(r_row, s, slice(0, 16), jnp.where(row_id == 9, skip_ref[...], jnp.exp(logs)), heads)

    pl.semaphore_wait(barrier, 7)
    for c in halos:
        c.start()

    code = lax.broadcasted_iota(jnp.int32, (8, GROUP), 0)
    table = jnp.concatenate([emb_ref[...].astype(f32), jnp.zeros((4, depth), f32)], axis=0).astype(bf)

    def looked(ids, flip):
        ids = 3 - ids if flip else ids
        n = ids.shape[1]
        hot = (code[:, :n] == jnp.broadcast_to(ids, (8, n))).astype(f32)
        return hot.T.astype(bf)

    for c in loads:
        c.wait()
    for j in range(blocks):
        wx_load(j).start()
    for s in range(2):
        for g in range(groups):
            hot = looked(ids_ref[:, g * GROUP : (g + 1) * GROUP], s == 1)
            rows = slice(starts[s] + g * GROUP, starts[s] + (g + 1) * GROUP)
            a_buf[rows] = (a_buf[rows].astype(f32) + mm(hot, table)).astype(bf)
    for c in halos:
        c.wait()
    hot = looked(ids_low[:, length - GROUP :], False)[GROUP - HALO :]
    rows = slice(0, HALO)
    a_buf[rows] = jnp.where(me > 0, a_buf[rows].astype(f32) + mm(hot, table), 0.0).astype(bf)
    hot = looked(ids_high[:, :GROUP], True)[:HALO]
    rows = slice(HALO + 2 * length, 2 * HALO + 2 * length)
    a_buf[rows] = jnp.where(me < count - 1, a_buf[rows].astype(f32) + mm(hot, table), 0.0).astype(bf)

    def spread_rows(ext, value):
        for p in range(2):
            ext[p] = value[:, p * half : (p + 1) * half]

    def conv(ext, s, g, tap_rows, bias):
        parts = []
        for p in range(2):
            lanes = slice(p * half, (p + 1) * half)
            total = jnp.broadcast_to(bias[:, lanes], (GROUP, half))
            for k in range(taps):
                shift = k - (taps - 1) if s == 0 else (taps - 1) - k
                start = starts[s] + g * GROUP + shift
                total = total + tap_rows[k : k + 1, lanes] * ext[p, start : start + GROUP]
            parts.append(total + total * jnp.tanh(total))
        return jnp.concatenate(parts, axis=1)

    head_row = lax.broadcasted_iota(jnp.int32, (2 * heads, BLOCK), 0) % heads
    head_lane = lax.broadcasted_iota(jnp.int32, (2 * heads, BLOCK), 1) // head_dim

    def spreader(j):
        return (head_row == head_lane + j * (BLOCK // head_dim)).astype(f32).astype(bf)

    def columns(j):
        return pl.ds(pl.multiple_of(j * BLOCK, BLOCK), BLOCK)

    def decay_of(a):
        return a[states : states + 1].astype(f32) + a[states + 1 : states + 2].astype(f32)

    def state_of(a):
        return a[0:states].astype(f32)

    def put(ref, at, s, state, decay):
        ref[at, s, 0:states] = state.astype(bf)
        high = decay.astype(bf)
        low = decay - high.astype(f32)
        pad_row = lax.broadcasted_iota(jnp.int32, (PAD, half), 0)
        ref[at, s, states : states + PAD] = jnp.where(pad_row == 0, high.astype(f32), low).astype(bf)

    def core_copy(b):
        return send(loc.at[b * 2 + 1 - core], core_in.at[b], core_s.at[b], core_r.at[b], seq=mate)

    def x_copy(b):
        return send(chip.at[b], x_in.at[b], x_s.at[b], x_r.at[b], seq=side)

    def z_copy(b, s):
        return send(z_out.at[b, s], z_in.at[b, s], z_s.at[b, s], z_r.at[b, s], seq=up if s == 0 else down)

    def ent_copy(b):
        span = pl.ds(pl.multiple_of(core * half, half), half)
        return send(ent_out.at[b], entry.at[b, :, :, span], ent_s.at[b], ent_r.at[b], seq=mate)

    def ent_arrived(b):
        span = pl.ds(pl.multiple_of((1 - core) * half, half), half)
        return send(ent_out.at[b], entry.at[b, :, :, span], ent_s.at[b], ent_r.at[b], seq=mate)

    def join(first, second, swapped):
        d1, d2 = decay_of(first), decay_of(second)
        s1, s2 = state_of(first), state_of(second)
        scale = jnp.where(swapped, d1, d2)
        state = jnp.where(swapped, scale * s2 + s1, scale * s1 + s2)
        return state, d1 * d2

    def chip_stage(b):
        core_copy(b).wait_recv()
        for s in range(2):
            mine, other = loc[b * 2 + core, s], core_in[b, s]
            swapped = (core == 1) if s == 0 else (core == 0)
            state, decay = join(mine, other, swapped)
            put(chip, b, s, state, decay)
        x_copy(b).start()

    def group_stage(b):
        x_copy(b).wait_recv()
        for s in range(2):
            swapped = (across == 1) if s == 0 else (across == 0)
            state, decay = join(chip[b, s], x_in[b, s], swapped)
            grp[b, s] = state
            grp_dec[b, s] = jnp.broadcast_to(decay, (8, half))
            z_out[b, s] = state.astype(bf)

            @pl.when(line == (0 if s == 0 else lines - 1))
            def _():
                z_copy(b, s).start()

    def line_stage(b, k):
        for s in range(2):
            at = k if s == 0 else lines - 1 - k

            @pl.when(line == at)
            def _():
                z_copy(b, s).wait_recv()
                if k < lines - 1:
                    state = grp_dec[b, s][0:1] * z_in[b, s].astype(f32) + grp[b, s]
                    z_out[b, s] = state.astype(bf)
                    z_copy(b, s).start()

    def enter_stage(b):
        for s in range(2):
            edge = line == (0 if s == 0 else lines - 1)
            entering = jnp.where(edge, 0.0, z_in[b, s].astype(f32))
            later_chip = (across == 1) if s == 0 else (across == 0)
            past = x_in[b, s]
            entering = jnp.where(later_chip, decay_of(past) * entering + state_of(past), entering)
            first = (core == 0) if s == 0 else (core == 1)
            mine, other = loc[b * 2 + core, s], core_in[b, s]
            dec = jnp.where(first, decay_of(mine), decay_of(other))
            adds = jnp.where(first, state_of(mine), state_of(other))
            second = dec * entering + adds
            span = pl.ds(pl.multiple_of(core * half, half), half)
            entry[b, s, :, span] = jnp.where(first, entering, second).astype(bf)
            ent_out[b, s] = jnp.where(first, second, entering).astype(bf)
        ent_copy(b).start()

    stages = [(2, chip_stage), (4, group_stage)]
    stages += [(4 + k, functools.partial(line_stage, k=k)) for k in range(1, lines)]
    stages += [(3 + lines, enter_stage)]

    def exchange(at):
        for lag, stage in stages:
            b = at - lag

            @pl.when((b >= 0) & (b < blocks))
            def _():
                stage(b)

    def project_x(j, ext):
        spread_rows(ext, mm(a_buf[...], w_buf[:, columns(j)]))

    def local_states(j, ext):
        cols = columns(j)
        spread_to = spreader(j)
        tap_rows, bias = 0.5 * tapx_ref[:, cols], 0.5 * biasx_ref[:, cols]
        for s in range(2):
            rows_at = mm(r_row[s], spread_to)
            state = None
            for g in range(groups) if s == 0 else range(groups - 1, -1, -1):
                rows = slice(g * GROUP, (g + 1) * GROUP)
                x = conv(ext, s, g, tap_rows, bias)
                x_buf[s, rows, cols] = x.astype(bf)
                xs = (x * mm(g_col[s, rows], spread_to)).astype(bf)
                xs_buf[s, rows, cols] = xs
                fresh = mm(bt_buf[s, g], xs)
                for p in (0, 1) if s == 0 else (1, 0):
                    c = 2 * g + p
                    part = fresh[p * states : (p + 1) * states]
                    if state is None:
                        st_buf[s, c, :, cols] = jnp.zeros((states, BLOCK), bf)
                        state = rows_at[c : c + 1] * part
                    else:
                        st_buf[s, c, :, cols] = state.astype(bf)
                        state = rows_at[c : c + 1] * (state + part)
            for p in range(2):
                lanes = slice(p * half, (p + 1) * half)
                put(loc, j * 2 + p, s, state[:, lanes], rows_at[8:9, lanes])
        core_copy(j).start()

    def two_blocks(i, _):
        j = 2 * i
        wx_load(j + 1).wait()
        exchange(j)
        project_x(j + 1, ext_odd)
        local_states(j, ext_even)
        wx_load(j + 2).wait()
        exchange(j + 1)
        project_x(j + 2, ext_even)
        local_states(j + 1, ext_odd)
        return 0

    wx_load(0).wait()
    spread_rows(ext_odd, mm(a_buf[...], wbc_buf[...]))
    project_x(0, ext_even)
    for s in range(2):
        keep = same & older[s]
        for g in range(groups):
            rows = slice(g * GROUP, (g + 1) * GROUP)
            both = conv(ext_odd, s, g, 0.5 * tapbc_ref[...], 0.5 * biasbc_ref[...])
            b, c = both[:, :states].astype(bf), both[:, states:].astype(bf)
            lh_buf[s, rows, 0:states] = c
            lh_buf[s, rows, states : states + GROUP] = jnp.where(keep, nt(c, b), 0.0).astype(bf)
            bt = b.astype(f32).T
            lower = r < SUB
            bt_buf[s, g, 0:states] = jnp.where(lower, bt, 0.0).astype(bf)
            bt_buf[s, g, states : 2 * states] = jnp.where(lower, 0.0, bt).astype(bf)

    lax.fori_loop(0, blocks // 2 - 1, two_blocks, 0)
    wx_load(blocks - 1).wait()
    wz_load.start()
    exchange(jnp.int32(blocks - 2))
    project_x(blocks - 1, ext_odd)
    local_states(blocks - 2, ext_even)
    wo_load.start()
    exchange(jnp.int32(blocks - 1))
    local_states(blocks - 1, ext_odd)

    def local_outputs(j, _):
        @pl.when((j == 0) | (j == 2) | (j == 5))
        def _():
            exchange(blocks + (j + 1) // 3)

        cols = columns(j)
        spread_to = spreader(j)
        for s in range(2):
            skip = mm(r_row[s], spread_to)[9:10]
            for g in range(groups):
                rows = slice(g * GROUP, (g + 1) * GROUP)
                factor = mm(f_col[s, rows], spread_to)
                xs = xs_buf[s, rows, cols]
                x = x_buf[s, rows, cols].astype(f32)
                ys = []
                for p in range(2):
                    c = 2 * g + p
                    rhs = jnp.concatenate([st_buf[s, c, :, cols], xs], axis=0)
                    ys.append(mm(lh_buf[s, c * SUB : (c + 1) * SUB], rhs))
                y = jnp.concatenate(ys, axis=0) * factor + skip * x
                x_buf[s, rows, cols] = y.astype(bf)
        return 0

    lax.fori_loop(0, blocks, local_outputs, 0)

    wz_load.wait()

    def gates(j, _):
        @pl.when((j == 0) | (j == 3) | (j == 6))
        def _():
            exchange(blocks + 3 + j // 3)

        cols = columns(j)
        h = 0.5 * mm(a_buf[HALO : HALO + 2 * length], wz_buf[:, cols])
        z = (h + h * jnp.tanh(h)).astype(bf)
        for s in range(2):
            xs_buf[s, :, cols] = z[s * length : (s + 1) * length]
        return 0

    lax.fori_loop(0, blocks, gates, 0)
    for at in range(blocks + 6, blocks + lines + 3):
        exchange(jnp.int32(at))
    for b in range(blocks):
        ent_arrived(b).wait_recv()
    wo_load.wait()

    def y_copy(i):
        return send(y_out.at[i], y_in.at[i], y_s.at[i], y_r.at[i], chan=other_chan)

    def rows_out(i, _):
        rows = pl.ds(pl.multiple_of(i * GROUP, GROUP), GROUP)

        def gate(j):
            cols = columns(j)
            spread_to = spreader(j)
            total = 0.0
            for s in range(2):
                carried = mm(lh_buf[s, rows, 0:states], entry[j, s])
                y = x_buf[s, rows, cols].astype(f32) + carried * mm(e_col[s, rows], spread_to)
                total = total + y * xs_buf[s, rows, cols].astype(f32)
            gated[:, cols] = total.astype(bf)

        def two_gates(n, _):
            gate(2 * n)
            gate(2 * n + 1)
            return 0

        lax.fori_loop(0, blocks // 2, two_gates, 0)

        def project(chan, target):
            cols = pl.ds(pl.multiple_of(chan * feats, BLOCK), feats)
            target[i] = mm(gated[...], w_buf[:, cols]).astype(bf)

        project(other_chan, y_out)
        y_copy(i).start()
        project(lane_mate, own)
        return 0

    lax.fori_loop(0, groups, rows_out, 0)

    for i in range(groups):
        y_copy(i).wait_recv()
        rows = slice(i * GROUP, (i + 1) * GROUP)
        out_ref[:, rows] = (own[i].astype(f32) + y_in[i].astype(f32)).T.astype(bf)

    for i in range(groups):
        y_copy(i).wait_send()
    for b in range(blocks):
        core_copy(b).wait_send()
        x_copy(b).wait_send()
        ent_copy(b).wait_send()

    @pl.when(line < lines - 1)
    def _():
        for b in range(blocks):
            z_copy(b, 0).wait_send()

    @pl.when(line > 0)
    def _():
        for b in range(blocks):
            z_copy(b, 1).wait_send()


def fused_device(
    hidden, nucleotides, base_embed, x_proj, gate_proj, bc_proj, conv_x, bias_x, conv_bc,
    bias_bc, log_decay, d_skip, out_proj,
):
    length, depth = hidden.shape[1:]
    inner = x_proj.shape[1]
    feats = out_proj.shape[1] // 2
    heads = d_skip.shape[0]
    states = conv_bc.shape[1] // 2
    blocks, groups, subs, half = inner // BLOCK, length // GROUP, length // SUB, BLOCK // 2
    rows = 2 * length + 2 * HALO
    bf, f32 = jnp.bfloat16, jnp.float32
    vmem, dma = pltpu.VMEM, pltpu.SemaphoreType.DMA
    small = pl.BlockSpec(memory_space=pltpu.VMEM)
    large = pl.BlockSpec(memory_space=pl.ANY)
    pair = (blocks, 2, states + PAD, half)
    out = pl.pallas_call(
        functools.partial(layer_kernel, inner // heads),
        out_shape=jax.ShapeDtypeStruct((feats, length), bf),
        in_specs=[small, large, small, large, large, large, large] + [small] * 6,
        out_specs=small,
        scratch_shapes=[
            vmem((rows, depth), bf),
            vmem((depth, inner), bf),
            vmem((depth, inner), bf),
            vmem((depth, 2 * states), bf),
            vmem((2, rows, BLOCK // 2), f32),
            vmem((2, rows, BLOCK // 2), f32),
            vmem((2, length, inner), bf),
            vmem((2, length, inner), bf),
            vmem((2, subs, states, inner), bf),
            vmem((2, length, states + GROUP), bf),
            vmem((2, groups, 2 * states, GROUP), bf),
            vmem((2, length, 2 * heads), bf),
            vmem((2, length, 2 * heads), bf),
            vmem((2, length, 2 * heads), bf),
            vmem((2, 16, 2 * heads), bf),
            vmem((1, length), jnp.int32),
            vmem((1, length), jnp.int32),
            vmem((2 * blocks, 2, states + PAD, half), bf),
            vmem(pair, bf),
            vmem(pair, bf),
            vmem(pair, bf),
            vmem((blocks, 2, states, half), f32),
            vmem((blocks, 2, 8, half), f32),
            vmem((blocks, 2, states, half), bf),
            vmem((blocks, 2, states, half), bf),
            vmem((blocks, 2, states, half), bf),
            vmem((blocks, 2, states, BLOCK), bf),
            vmem((GROUP, inner), bf),
            vmem((groups, GROUP, feats), bf),
            vmem((groups, GROUP, feats), bf),
            vmem((groups, GROUP, feats), bf),
            dma((5,)), dma((blocks,)), dma((4,)), dma((4,)),
            dma((blocks,)), dma((blocks,)), dma((blocks,)), dma((blocks,)),
            dma((blocks, 2)), dma((blocks, 2)), dma((blocks,)), dma((blocks,)),
            dma((groups,)), dma((groups,)),
        ],
        compiler_params=pltpu.CompilerParams(
            collective_id=0, has_side_effects=True, vmem_limit_bytes=67043328
        ),
        name="layer",
    )(
        nucleotides[None], hidden, base_embed, x_proj, gate_proj, bc_proj, out_proj, conv_x, bias_x[None], conv_bc,
        bias_bc[None], log_decay, d_skip[None],
    )
    return out


def any_device(*args):
    hidden, x_proj, conv_bc = args[0], args[3], args[8]
    fits = lax.axis_size("chan") == 2 and lax.axis_size("seq") % 4 == 0 and lax.axis_size("seq") >= 8
    fits = fits and hidden.shape[1] == 8 * SUB and conv_bc.shape[1] == BLOCK
    fits = fits and x_proj.shape[1] % (2 * BLOCK) == 0 and x_proj.shape[1] >= 8 * BLOCK
    return fused_device(*args) if fits else per_device(*args)


def solution(mesh):
    in_specs = (
        P(None, "seq", None), P("seq"), P(), P(None, "chan"), P(None, "chan"), P(),
        P(None, "chan"), P("chan"), P(), P(), P(None, "chan", "seq"), P("chan"), P("chan", None),
    )
    return jax.shard_map(
        any_device, mesh=mesh, in_specs=in_specs, out_specs=P("chan", "seq"), check_vma=False
    )
```

```python
import functools

import jax
import jax.numpy as jnp
from jax import lax
from jax.experimental import pallas as pl
from jax.experimental.pallas import tpu as pltpu
from jax.sharding import PartitionSpec as P

CHUNK = 128
WIDTH = 256
PAD = 16
LOG2E = 1.4426950408889634
MESH = pl.DeviceIdType.MESH


def silu(v):
    return v * (0.5 + 0.5 * jnp.tanh(0.5 * v))


def strand_inputs(hidden_rows, ids, base_embed):
    table = base_embed.astype(jnp.float32)
    pick = ids[:, None]
    low = jnp.where(pick == 0, table[0], table[1])
    high = jnp.where(pick == 2, table[2], table[3])
    looked = jnp.where(pick < 2, low, high)
    return (hidden_rows.astype(jnp.float32) + looked).astype(jnp.bfloat16)


def spread(cols, first, heads, head_dim):
    rows = cols.shape[0]
    per = 128 // head_dim
    lane = lax.broadcasted_iota(jnp.int32, (rows, 128), 1)
    tiles = []
    for t in range(heads // per):
        tile = jnp.broadcast_to(cols[:, first + t * per : first + t * per + 1], (rows, 128))
        for p in range(1, per):
            h = first + t * per + p
            tile = jnp.where(
                lane >= p * head_dim, jnp.broadcast_to(cols[:, h : h + 1], (rows, 128)), tile
            )
        tiles.append(tile)
    return jnp.concatenate(tiles, axis=1)


def state_kernel(head_dim, x_ref, rim_ref, taps_ref, bias_ref, tail_ref, decay_ref, bt_ref, conv_ref, state_ref, ext):
    strands, length, width = x_ref.shape
    taps = taps_ref.shape[0]
    heads = width // head_dim
    for s in range(strands):
        ext[8 : 8 + length] = x_ref[s].astype(jnp.float32)
        if s == 0:
            ext[0:8] = rim_ref[s].astype(jnp.float32)
        else:
            ext[8 + length : 16 + length] = rim_ref[s].astype(jnp.float32)
        chunks = length // CHUNK
        for step in range(chunks):
            c = step if s == 0 else chunks - 1 - step
            total = jnp.broadcast_to(bias_ref[...], (CHUNK, width))
            for k in range(taps):
                shift = k - (taps - 1) if s == 0 else (taps - 1) - k
                start = 8 + c * CHUNK + shift
                total = total + taps_ref[k : k + 1] * ext[start : start + CHUNK]
            rows = slice(c * CHUNK, (c + 1) * CHUNK)
            x = silu(total).astype(jnp.bfloat16)
            conv_ref[s, rows] = x
            scale = spread(tail_ref[0, rows], s * heads, heads, head_dim)
            xs = (x.astype(jnp.float32) * scale).astype(jnp.bfloat16)
            part = jnp.dot(bt_ref[s, :, rows], xs, preferred_element_type=jnp.float32)
            if step == 0:
                acc = part
            else:
                acc = acc + part
        states = acc.shape[0]
        state_ref[s, :states] = acc.astype(state_ref.dtype)
        state_ref[s, states:] = jnp.broadcast_to(
            decay_ref[s : s + 1], (PAD, width)
        ).astype(state_ref.dtype)


def scan_kernel(head_dim, s, x_ref, cols_ref, rows_ref, bt_ref, c_ref, chunk_ref, skip_ref, out_ref, scores):
    _, length, width = x_ref.shape
    heads = width // head_dim
    per = 128 // head_dim
    chunks = length // CHUNK

    @pl.when(pl.program_id(0) == 0)
    def _():
        t = lax.broadcasted_iota(jnp.int32, (CHUNK, CHUNK), 0)
        r = lax.broadcasted_iota(jnp.int32, (CHUNK, CHUNK), 1)
        keep = (r <= t) if s == 0 else (r >= t)
        for c in range(chunks):
            rows = slice(c * CHUNK, (c + 1) * CHUNK)
            sc = jnp.dot(c_ref[s, rows], bt_ref[s, :, rows], preferred_element_type=jnp.float32)
            scores[c] = jnp.where(keep, sc, 0.0)

    lane = lax.broadcasted_iota(jnp.int32, (CHUNK, 128), 1)
    state = None
    order = range(chunks) if s == 0 else range(chunks - 1, -1, -1)
    for step, c in enumerate(order):
        rows = slice(c * CHUNK, (c + 1) * CHUNK)
        cols = cols_ref[0, rows]
        base = s * 3 * heads
        x = x_ref[0, rows]
        sc = scores[c]
        y = skip_ref[...] * x.astype(jnp.float32)
        if step > 0:
            carried = jnp.dot(
                c_ref[s, rows], state.astype(jnp.bfloat16), preferred_element_type=jnp.float32
            )
            y = y + carried * spread(cols, base + heads, heads, head_dim)
        tiles = []
        for t in range(heads // per):
            xt = x[:, t * 128 : (t + 1) * 128]
            lhs, rhs = [], []
            for p in range(per):
                h = t * per + p
                gap = cols[:, base + h : base + h + 1] + rows_ref[0, s * heads + h : s * heads + h + 1, rows]
                lhs.append((sc * jnp.exp2(jnp.minimum(gap, 0.0))).astype(jnp.bfloat16))
                inside = (lane >= p * head_dim) & (lane < (p + 1) * head_dim)
                rhs.append(jnp.where(inside, xt, jnp.zeros_like(xt)))
            tiles.append(
                jnp.dot(
                    jnp.concatenate(lhs, axis=1),
                    jnp.concatenate(rhs, axis=0),
                    preferred_element_type=jnp.float32,
                )
            )
        y = y + jnp.concatenate(tiles, axis=1)
        out_ref[rows] = y.astype(out_ref.dtype)
        if step < chunks - 1:
            scale = spread(cols, base + 2 * heads, heads, head_dim)
            xs = (x.astype(jnp.float32) * scale).astype(jnp.bfloat16)
            fresh = jnp.dot(bt_ref[s, :, rows], xs, preferred_element_type=jnp.float32)
            at = s * chunks + c
            state = fresh if step == 0 else chunk_ref[at : at + 1] * state + fresh


def gate_kernel(head_dim, y_zero, y_one, z_ref, entry_ref, c_ref, in_ref, out_ref):
    strands, length, width = z_ref.shape
    y_refs = (y_zero, y_one)
    heads = width // head_dim
    for c in range(length // CHUNK):
        rows = slice(c * CHUNK, (c + 1) * CHUNK)
        total = 0.0
        for s in range(strands):
            carried = jnp.dot(c_ref[s, rows], in_ref[s], preferred_element_type=jnp.float32)
            y = y_refs[s][rows].astype(jnp.float32)
            y = y + carried * spread(entry_ref[0, rows], s * heads, heads, head_dim)
            total = total + y * silu(z_ref[s, rows].astype(jnp.float32))
        out_ref[rows] = total.astype(out_ref.dtype)


def neighbours(low_rows, high_rows):
    count = lax.axis_size("seq")
    forward = [(i, i + 1) for i in range(count - 1)]
    backward = [(i + 1, i) for i in range(count - 1)]
    return lax.ppermute(low_rows, "seq", forward), lax.ppermute(high_rows, "seq", backward)


def entering(local, states, across_work, line_work):
    count = lax.axis_size("seq")
    me = lax.axis_index("seq")
    half = local.shape[2] // 2
    core, across = me % 2, (me // 2) % 2
    row = lax.broadcasted_iota(jnp.int32, (1, local.shape[1], 1), 1)

    def decay(a):
        return a[..., states : states + 1, :].astype(jnp.float32)

    def joined(first, second, second_is_earlier):
        flag = second_is_earlier[:, None, None]
        a = jnp.where(flag, 1.0, decay(second))
        b = jnp.where(flag, decay(first), 1.0)
        first, second = first.astype(jnp.float32), second.astype(jnp.float32)
        both = jnp.where(row < states, a * first + b * second, first * second)
        return both.astype(jnp.bfloat16)

    def after(state, step, is_earlier):
        moved = decay(step) * state + step[..., :states, :].astype(jnp.float32)
        return jnp.where(is_earlier[:, None, None], moved, state)

    def mine(a):
        return lax.dynamic_slice_in_dim(a, core * half, half, a.ndim - 1)

    swap = [(i, i ^ 1) for i in range(count)]
    swap_pair = [(i, i ^ 2) for i in range(count)]
    up = [(i, i + 4) for i in range(count - 4)]
    down = [(i + 4, i) for i in range(count - 4)]

    other = lax.ppermute(local, "seq", swap)
    core_earlier = jnp.stack([core == 1, core == 0])
    chip = joined(mine(local), mine(other), core_earlier)
    chip_other = lax.ppermute(chip, "seq", swap_pair)
    results = []

    def beside(work, before, arrived):
        arrived, out = lax.optimization_barrier((arrived, work(before)))
        results.append(out)
        return arrived

    chip_other = beside(across_work, chip, chip_other)
    pair_earlier = jnp.stack([across == 1, across == 0])
    group = joined(chip, chip_other, pair_earlier)
    moving = [group[0], group[1]]
    total = [0.0, 0.0]
    factor = [1.0, 1.0]
    for step in range(count // 4 - 1):
        before = moving
        moving = [lax.ppermute(moving[0], "seq", up), lax.ppermute(moving[1], "seq", down)]
        if step < len(line_work):
            moving = beside(line_work[step], before, moving)
        for s in range(2):
            total[s] = total[s] + factor[s] * moving[s][:states].astype(jnp.float32)
            factor[s] = factor[s] * decay(moving[s])
    shape = (states, half)
    total = jnp.stack([jnp.broadcast_to(jnp.asarray(t, jnp.float32), shape) for t in total])
    chip_in = after(total, chip_other, pair_earlier).astype(jnp.bfloat16)
    rest = lax.ppermute(chip_in, "seq", swap)
    low = jnp.where(core == 0, chip_in, rest)
    high = jnp.where(core == 0, rest, chip_in)
    full = jnp.concatenate([low, high], axis=2).astype(jnp.float32)
    for work in line_work[max(count // 4 - 1, 0) :]:
        results.append(work(moving))
    return after(full, other, core_earlier).astype(jnp.bfloat16), results


def per_device(
    hidden, nucleotides, base_embed, x_proj, gate_proj, bc_proj, conv_x, bias_x, conv_bc,
    bias_bc, log_decay, d_skip, out_proj,
):
    taps, inner = conv_x.shape
    length = hidden.shape[1]
    head_count = d_skip.shape[0]
    head_dim = inner // head_count
    states = conv_bc.shape[1] // 2
    width = min(WIDTH, inner)
    blocks = inner // width
    heads = width // head_dim
    chunks = length // CHUNK
    inv_root = states ** (-0.5)

    r = jnp.arange(length)
    rates = log_decay.astype(jnp.float32)
    same = (r[:, None] // CHUNK) == (r[None, :] // CHUNK)
    older = [r[:, None] <= r[None, :], r[:, None] >= r[None, :]]

    def sums(masks):
        return jnp.stack(
            [
                jnp.dot(log_decay[s], masks[s].astype(jnp.bfloat16), preferred_element_type=jnp.float32)
                for s in range(2)
            ]
        )

    cum = sums([same & older[0], same & older[1]])
    left = sums([same & (r[:, None] > r[None, :]), same & (r[:, None] < r[None, :])])
    part = length // 2
    cum_all = sums(older)
    left_all = sums([r[:, None] > r[None, :], r[:, None] < r[None, :]])
    inject = jnp.sqrt(-jnp.expm1(2.0 * rates))
    tail_all = jnp.exp(left_all) * inject
    tail = jnp.exp(left) * inject
    entry = jnp.exp(cum) * inv_root
    row_terms = jnp.log2(inject * inv_root) - cum * LOG2E
    rows_arr = row_terms.reshape(2, blocks, heads, length).transpose(1, 0, 2, 3)
    rows_arr = rows_arr.reshape(blocks, 2 * heads, length)
    cols_arr = jnp.stack([cum * LOG2E, entry, tail], axis=1)
    cols_arr = cols_arr.reshape(2, 3, blocks, heads, length).transpose(2, 4, 0, 1, 3)
    cols_arr = cols_arr.reshape(blocks, length, 6 * heads)
    tail_arr = tail_all.reshape(2, blocks, heads, length).transpose(1, 3, 0, 2)
    tail_arr = tail_arr.reshape(blocks, length, 2 * heads)
    span_logs = jnp.sum(rates.reshape(2, head_count, chunks, CHUNK), axis=3)
    span_logs = jnp.repeat(span_logs.transpose(0, 2, 1), head_dim, axis=2)
    chunk_decay = jnp.exp(span_logs).reshape(2 * chunks, inner)
    shard_decay = jnp.exp(jnp.sum(span_logs, axis=1))
    entry_all = jnp.exp(cum_all) * inv_root
    entry_arr = entry_all.reshape(2, blocks, heads, length).transpose(1, 3, 0, 2)
    entry_arr = entry_arr.reshape(blocks, length, 2 * heads)
    skip = jnp.repeat(d_skip, head_dim)[None]

    inputs = jnp.concatenate(
        [
            strand_inputs(hidden[0], nucleotides, base_embed),
            strand_inputs(hidden[1], 3 - nucleotides, base_embed),
        ],
        axis=0,
    )
    inputs = lax.optimization_barrier(inputs)

    def project(weight):
        out = jnp.dot(inputs, weight, preferred_element_type=jnp.float32)
        return out.astype(jnp.bfloat16).reshape(2, length, -1)

    bc_pre = project(bc_proj)
    x_pre = project(x_proj)
    edge = taps - 1
    low = jnp.concatenate([x_pre[0, -edge:], bc_pre[0, -edge:]], axis=1)
    high = jnp.concatenate([x_pre[1, :edge], bc_pre[1, :edge]], axis=1)
    low, high = neighbours(low, high)
    x_rim = jnp.stack(
        [
            jnp.pad(low[:, :inner], ((8 - edge, 0), (0, 0))),
            jnp.pad(high[:, :inner], ((0, 8 - edge), (0, 0))),
        ]
    )
    bc_ext = [
        jnp.concatenate([low[:, inner:], bc_pre[0]], axis=0),
        jnp.concatenate([bc_pre[1], high[:, inner:]], axis=0),
    ]
    bc_conv = []
    for s in range(2):
        total = bias_bc
        for k in range(taps):
            at = k if s == 0 else edge - k
            total = total + conv_bc[k] * bc_ext[s][at : at + length].astype(jnp.float32)
        bc_conv.append(jax.nn.silu(total).astype(jnp.bfloat16))
    bc_conv = jnp.stack(bc_conv)
    c_rows = bc_conv[..., states:]
    b_cols = bc_conv[..., :states].transpose(0, 2, 1)

    params = pltpu.CompilerParams(dimension_semantics=("arbitrary",), vmem_limit_bytes=48 * 1024 * 1024)
    wide = pl.BlockSpec((2, length, width), lambda i: (0, 0, i))
    state_block = pl.BlockSpec((2, states, width), lambda i: (0, 0, i))
    whole = lambda a: pl.BlockSpec(a.shape, lambda i: (0,) * a.ndim)
    x_conv, local = pl.pallas_call(
        functools.partial(state_kernel, head_dim),
        grid=(blocks,),
        out_shape=(
            jax.ShapeDtypeStruct((2, length, inner), jnp.bfloat16),
            jax.ShapeDtypeStruct((2, states + PAD, inner), jnp.bfloat16),
        ),
        in_specs=[
            wide,
            pl.BlockSpec((2, 8, width), lambda i: (0, 0, i)),
            pl.BlockSpec((taps, width), lambda i: (0, i)),
            pl.BlockSpec((1, width), lambda i: (0, i)),
            pl.BlockSpec((1, length, 2 * heads), lambda i: (i, 0, 0)),
            pl.BlockSpec((2, width), lambda i: (0, i)),
            whole(b_cols),
        ],
        out_specs=(wide, pl.BlockSpec((2, states + PAD, width), lambda i: (0, 0, i))),
        scratch_shapes=[pltpu.VMEM((length + 16, width), jnp.float32)],
        compiler_params=params,
        name="conv_state",
    )(x_pre, x_rim, conv_x, bias_x[None], tail_arr, shard_decay, b_cols)

    def gate_rows(before):
        rows, _ = lax.optimization_barrier((inputs, before))
        out = jnp.dot(rows, gate_proj, preferred_element_type=jnp.float32)
        return out.astype(jnp.bfloat16).reshape(2, length, -1)

    def scan_strand(strand, before):
        x_in, _ = lax.optimization_barrier((x_conv, before))
        return pl.pallas_call(
        functools.partial(scan_kernel, head_dim, strand),
        grid=(blocks,),
        out_shape=jax.ShapeDtypeStruct((length, inner), jnp.bfloat16),
        in_specs=[
            pl.BlockSpec((1, length, width), lambda i: (strand, 0, i)),
            pl.BlockSpec((1, length, 6 * heads), lambda i: (i, 0, 0)),
            pl.BlockSpec((1, 2 * heads, length), lambda i: (i, 0, 0)),
            whole(b_cols),
            whole(c_rows),
            pl.BlockSpec((2 * chunks, width), lambda i: (0, i)),
            pl.BlockSpec((1, width), lambda i: (0, i)),
        ],
        out_specs=pl.BlockSpec((length, width), lambda i: (0, i)),
        scratch_shapes=[pltpu.VMEM((chunks, CHUNK, CHUNK), jnp.float32)],
        compiler_params=params,
        cost_estimate=pl.CostEstimate(
            flops=12 * length * inner * states, bytes_accessed=6 * length * inner, transcendentals=0
        ),
        name="scan",
    )(x_in, cols_arr, rows_arr, b_cols, c_rows, chunk_decay, skip)

    incoming, (z_pre, y_zero, y_one) = entering(
        local,
        states,
        gate_rows,
        [functools.partial(scan_strand, 0), functools.partial(scan_strand, 1)],
    )

    def scan_half(half, before=None):
        entered = incoming
        if before is not None:
            entered, _ = lax.optimization_barrier((incoming, before))
        rows_spec = pl.BlockSpec((2, part, width), lambda i: (0, half, i))
        return pl.pallas_call(
            functools.partial(gate_kernel, head_dim),
            grid=(blocks,),
            out_shape=jax.ShapeDtypeStruct((part, inner), jnp.bfloat16),
            in_specs=[
                pl.BlockSpec((part, width), lambda i: (half, i)),
                pl.BlockSpec((part, width), lambda i: (half, i)),
                rows_spec,
                pl.BlockSpec((1, part, 2 * heads), lambda i: (i, half, 0)),
                pl.BlockSpec((2, part, states), lambda i: (0, half, 0)),
                state_block,
            ],
            out_specs=pl.BlockSpec((part, width), lambda i: (0, i)),
            compiler_params=params,
            cost_estimate=pl.CostEstimate(
                flops=96 * part * inner * states, bytes_accessed=48 * part * inner, transcendentals=0
            ),
            name="gate",
        )(y_zero, y_one, z_pre, entry_arr, c_rows, entered)

    def out_part(weight, rows):
        return lax.dot_general(
            weight, rows, (((0,), (1,)), ((), ())), preferred_element_type=jnp.float32
        ).astype(jnp.bfloat16)

    if lax.axis_size("chan") == 2:
        size = out_proj.shape[1] // 2
        mine = lax.axis_index("chan")
        send_weight = lax.dynamic_slice_in_dim(out_proj, (1 - mine) * size, size, 1)
        own_weight = lax.dynamic_slice_in_dim(out_proj, mine * size, size, 1)
        first = scan_half(0)
        part_first = out_part(send_weight, first)
        sent_first = lax.ppermute(part_first, "chan", [(0, 1), (1, 0)])
        second = scan_half(1, part_first)
        sent_first, second = lax.optimization_barrier((sent_first, second))
        sent_second = lax.ppermute(out_part(send_weight, second), "chan", [(0, 1), (1, 0)])
        own = lax.optimization_barrier(out_part(own_weight, jnp.concatenate([first, second])))
        sent = jnp.concatenate([sent_first, sent_second], axis=1)
        return (own.astype(jnp.float32) + sent.astype(jnp.float32)).astype(jnp.bfloat16)
    mixed_in = jnp.concatenate([scan_half(0), scan_half(1)])
    return lax.psum_scatter(
        out_part(out_proj, mixed_in), "chan", scatter_dimension=0, tiled=True
    )


GROUP = 128
SUB = 64
HALO = 16
BLOCK = 256


def split_store(ref, s, rows, value, heads):
    high = value.astype(jnp.bfloat16)
    ref[s, rows, 0:heads] = high
    ref[s, rows, heads : 2 * heads] = (value - high.astype(jnp.float32)).astype(jnp.bfloat16)


def one_minus_exp(u):
    small = -u * (1 + u / 2 * (1 + u / 3 * (1 + u / 4 * (1 + u / 5 * (1 + u / 6)))))
    return jnp.where(u > -0.25, small, 1.0 - jnp.exp(u))


def nt(a, b):
    return lax.dot_general(a, b, (((1,), (1,)), ((), ())), preferred_element_type=jnp.float32)


def mm(a, b):
    return jnp.dot(a, b, preferred_element_type=jnp.float32)


def layer_kernel(
    head_dim, ids_ref, hid_ref, emb_ref, wx_hbm, wz_hbm, wbc_hbm, wo_hbm, tapx_ref, biasx_ref, tapbc_ref, biasbc_ref,
    ld_ref, skip_ref, out_ref,
    a_buf, w_buf, wz_buf, wbc_buf, ext_even, ext_odd, x_buf, xs_buf, st_buf, lh_buf, bt_buf, g_col, f_col, e_col, r_row,
    ids_low, ids_high, loc, core_in, chip, x_in, grp, grp_dec, z_out, z_in, ent_out, entry, gated, y_out, y_in, own,
    load_sem, wx_sem, halo_s, halo_r, core_s, core_r, x_s, x_r, z_s, z_r, ent_s, ent_r, y_s, y_r,
):
    _, length, depth = hid_ref.shape
    inner = wx_hbm.shape[1]
    feats = wo_hbm.shape[1] // 2
    taps = tapx_ref.shape[0]
    heads = inner // head_dim
    states = tapbc_ref.shape[1] // 2
    blocks = inner // BLOCK
    half = BLOCK // 2
    groups = length // GROUP
    subs = length // SUB
    inv_root = states ** (-0.5)
    bf, f32 = jnp.bfloat16, jnp.float32
    starts = (HALO, HALO + length)

    count = lax.axis_size("seq")
    me = lax.axis_index("seq")
    lane_mate = lax.axis_index("chan")
    core, across, line = me % 2, (me // 2) % 2, me // 4
    lines = count // 4
    right, left = (me + 1) % count, (me + count - 1) % count
    mate = me + 1 - 2 * core
    side = me + 2 - 4 * across
    up, down = (me + 4) % count, (me + count - 4) % count
    other_chan = 1 - lane_mate

    loads = [
        pltpu.make_async_copy(hid_ref.at[0], a_buf.at[pl.ds(starts[0], length)], load_sem.at[0]),
        pltpu.make_async_copy(hid_ref.at[1], a_buf.at[pl.ds(starts[1], length)], load_sem.at[1]),
        pltpu.make_async_copy(wbc_hbm, wbc_buf, load_sem.at[2]),
    ]

    def wx_load(j):
        cols = pl.ds(pl.multiple_of(j * BLOCK, BLOCK), BLOCK)
        return pltpu.make_async_copy(wx_hbm.at[:, cols], w_buf.at[:, cols], wx_sem.at[j])

    wz_load = pltpu.make_async_copy(wz_hbm, wz_buf, load_sem.at[3])
    wo_load = pltpu.make_async_copy(wo_hbm, w_buf, load_sem.at[4])
    for c in loads:
        c.start()

    barrier = pltpu.get_barrier_semaphore()
    for peer in (right, left, mate, side, up, down):
        pl.semaphore_signal(barrier, inc=1, device_id={"seq": peer}, device_id_type=MESH)
    pl.semaphore_signal(barrier, inc=1, device_id={"chan": other_chan}, device_id_type=MESH)
    def send(src, dst, s_sem, r_sem, **where):
        return pltpu.make_async_remote_copy(
            src_ref=src, dst_ref=dst, send_sem=s_sem, recv_sem=r_sem, device_id=where, device_id_type=MESH
        )

    halos = [
        send(hid_ref.at[0, pl.ds(length - HALO, HALO)], a_buf.at[pl.ds(0, HALO)], halo_s.at[0], halo_r.at[0], seq=right),
        send(hid_ref.at[1, pl.ds(0, HALO)], a_buf.at[pl.ds(HALO + 2 * length, HALO)], halo_s.at[1], halo_r.at[1], seq=left),
        send(ids_ref, ids_low, halo_s.at[2], halo_r.at[2], seq=right),
        send(ids_ref, ids_high, halo_s.at[3], halo_r.at[3], seq=left),
    ]

    t = lax.broadcasted_iota(jnp.int32, (GROUP, GROUP), 0)
    r = lax.broadcasted_iota(jnp.int32, (GROUP, GROUP), 1)
    same = (t // SUB) == (r // SUB)
    low_half = (r % SUB) < (SUB // 2)
    older = (r <= t, r >= t)
    first_half = (low_half, jnp.logical_not(low_half))
    eye = (t == r).astype(f32)
    row = lax.broadcasted_iota(jnp.int32, (16, length), 0)
    pos = lax.broadcasted_iota(jnp.int32, (16, length), 1)
    row_id = lax.broadcasted_iota(jnp.int32, (16, heads), 0)
    in_low = ((pos % SUB) < (SUB // 2)).astype(f32)
    for s in range(2):
        q_mask = jnp.where(same, older[s].astype(f32) - first_half[s].astype(f32), 0.0)
        masks = jnp.concatenate([q_mask, older[s].astype(f32), eye], axis=0).astype(bf)
        before = jnp.zeros((1, heads), f32)
        for g in range(groups) if s == 0 else range(groups - 1, -1, -1):
            rows = slice(g * GROUP, (g + 1) * GROUP)
            res = nt(masks, ld_ref[s, :, rows])
            q, cum, rate = res[0:GROUP], res[GROUP : 2 * GROUP], res[2 * GROUP :]
            inject = jnp.sqrt(one_minus_exp(2.0 * rate))
            split_store(g_col, s, rows, jnp.exp(-q) * inject, heads)
            split_store(f_col, s, rows, jnp.exp(q) * inv_root, heads)
            cum = cum + before
            split_store(e_col, s, rows, jnp.exp(cum) * inv_root, heads)
            before = cum[GROUP - 1 :] if s == 0 else cum[0:1]
        first = in_low if s == 0 else 1.0 - in_low
        here = ((pos // SUB) == row).astype(f32)
        after = ((pos // SUB) == (row + 1 if s == 0 else row - 1)).astype(f32)
        pick = jnp.where(row < 8, here * (1.0 - first) + after * first, 1.0)
        logs = nt(pick.astype(bf), ld_ref[s])
        split_store(r_row, s, slice(0, 16), jnp.where(row_id == 9, skip_ref[...], jnp.exp(logs)), heads)

    pl.semaphore_wait(barrier, 7)
    for c in halos:
        c.start()

    code = lax.broadcasted_iota(jnp.int32, (8, GROUP), 0)
    table = jnp.concatenate([emb_ref[...].astype(f32), jnp.zeros((4, depth), f32)], axis=0).astype(bf)

    def looked(ids, flip):
        ids = 3 - ids if flip else ids
        n = ids.shape[1]
        hot = (code[:, :n] == jnp.broadcast_to(ids, (8, n))).astype(f32)
        return hot.T.astype(bf)

    for c in loads:
        c.wait()
    for j in range(blocks):
        wx_load(j).start()
    for s in range(2):
        for g in range(groups):
            hot = looked(ids_ref[:, g * GROUP : (g + 1) * GROUP], s == 1)
            rows = slice(starts[s] + g * GROUP, starts[s] + (g + 1) * GROUP)
            a_buf[rows] = (a_buf[rows].astype(f32) + mm(hot, table)).astype(bf)
    for c in halos:
        c.wait()
    hot = looked(ids_low[:, length - GROUP :], False)[GROUP - HALO :]
    rows = slice(0, HALO)
    a_buf[rows] = jnp.where(me > 0, a_buf[rows].astype(f32) + mm(hot, table), 0.0).astype(bf)
    hot = looked(ids_high[:, :GROUP], True)[:HALO]
    rows = slice(HALO + 2 * length, 2 * HALO + 2 * length)
    a_buf[rows] = jnp.where(me < count - 1, a_buf[rows].astype(f32) + mm(hot, table), 0.0).astype(bf)

    def spread_rows(ext, value):
        for p in range(2):
            ext[p] = value[:, p * half : (p + 1) * half]

    def conv(ext, s, g, tap_rows, bias):
        parts = []
        for p in range(2):
            lanes = slice(p * half, (p + 1) * half)
            total = jnp.broadcast_to(bias[:, lanes], (GROUP, half))
            for k in range(taps):
                shift = k - (taps - 1) if s == 0 else (taps - 1) - k
                start = starts[s] + g * GROUP + shift
                total = total + tap_rows[k : k + 1, lanes] * ext[p, start : start + GROUP]
            parts.append(total + total * jnp.tanh(total))
        return jnp.concatenate(parts, axis=1)

    head_row = lax.broadcasted_iota(jnp.int32, (2 * heads, BLOCK), 0) % heads
    head_lane = lax.broadcasted_iota(jnp.int32, (2 * heads, BLOCK), 1) // head_dim

    def spreader(j):
        return (head_row == head_lane + j * (BLOCK // head_dim)).astype(f32).astype(bf)

    def columns(j):
        return pl.ds(pl.multiple_of(j * BLOCK, BLOCK), BLOCK)

    def decay_of(a):
        return a[states : states + 1].astype(f32) + a[states + 1 : states + 2].astype(f32)

    def state_of(a):
        return a[0:states].astype(f32)

    def put(ref, at, s, state, decay):
        ref[at, s, 0:states] = state.astype(bf)
        high = decay.astype(bf)
        low = decay - high.astype(f32)
        pad_row = lax.broadcasted_iota(jnp.int32, (PAD, half), 0)
        ref[at, s, states : states + PAD] = jnp.where(pad_row == 0, high.astype(f32), low).astype(bf)

    def core_copy(b):
        return send(loc.at[b * 2 + 1 - core], core_in.at[b], core_s.at[b], core_r.at[b], seq=mate)

    def x_copy(b):
        return send(chip.at[b], x_in.at[b], x_s.at[b], x_r.at[b], seq=side)

    def z_copy(b, s):
        return send(z_out.at[b, s], z_in.at[b, s], z_s.at[b, s], z_r.at[b, s], seq=up if s == 0 else down)

    def ent_copy(b):
        span = pl.ds(pl.multiple_of(core * half, half), half)
        return send(ent_out.at[b], entry.at[b, :, :, span], ent_s.at[b], ent_r.at[b], seq=mate)

    def ent_arrived(b):
        span = pl.ds(pl.multiple_of((1 - core) * half, half), half)
        return send(ent_out.at[b], entry.at[b, :, :, span], ent_s.at[b], ent_r.at[b], seq=mate)

    def join(first, second, swapped):
        d1, d2 = decay_of(first), decay_of(second)
        s1, s2 = state_of(first), state_of(second)
        scale = jnp.where(swapped, d1, d2)
        state = jnp.where(swapped, scale * s2 + s1, scale * s1 + s2)
        return state, d1 * d2

    def chip_stage(b):
        core_copy(b).wait_recv()
        for s in range(2):
            mine, other = loc[b * 2 + core, s], core_in[b, s]
            swapped = (core == 1) if s == 0 else (core == 0)
            state, decay = join(mine, other, swapped)
            put(chip, b, s, state, decay)
        x_copy(b).start()

    def group_stage(b):
        x_copy(b).wait_recv()
        for s in range(2):
            swapped = (across == 1) if s == 0 else (across == 0)
            state, decay = join(chip[b, s], x_in[b, s], swapped)
            grp[b, s] = state
            grp_dec[b, s] = jnp.broadcast_to(decay, (8, half))
            z_out[b, s] = state.astype(bf)

            @pl.when(line == (0 if s == 0 else lines - 1))
            def _():
                z_copy(b, s).start()

    def line_stage(b, k):
        for s in range(2):
            at = k if s == 0 else lines - 1 - k

            @pl.when(line == at)
            def _():
                z_copy(b, s).wait_recv()
                if k < lines - 1:
                    state = grp_dec[b, s][0:1] * z_in[b, s].astype(f32) + grp[b, s]
                    z_out[b, s] = state.astype(bf)
                    z_copy(b, s).start()

    def enter_stage(b):
        for s in range(2):
            edge = line == (0 if s == 0 else lines - 1)
            entering = jnp.where(edge, 0.0, z_in[b, s].astype(f32))
            later_chip = (across == 1) if s == 0 else (across == 0)
            past = x_in[b, s]
            entering = jnp.where(later_chip, decay_of(past) * entering + state_of(past), entering)
            first = (core == 0) if s == 0 else (core == 1)
            mine, other = loc[b * 2 + core, s], core_in[b, s]
            dec = jnp.where(first, decay_of(mine), decay_of(other))
            adds = jnp.where(first, state_of(mine), state_of(other))
            second = dec * entering + adds
            span = pl.ds(pl.multiple_of(core * half, half), half)
            entry[b, s, :, span] = jnp.where(first, entering, second).astype(bf)
            ent_out[b, s] = jnp.where(first, second, entering).astype(bf)
        ent_copy(b).start()

    stages = [(2, chip_stage), (4, group_stage)]
    stages += [(4 + k, functools.partial(line_stage, k=k)) for k in range(1, lines)]
    stages += [(3 + lines, enter_stage)]

    def exchange(at):
        for lag, stage in stages:
            b = at - lag

            @pl.when((b >= 0) & (b < blocks))
            def _():
                stage(b)

    def project_x(j, ext):
        spread_rows(ext, mm(a_buf[...], w_buf[:, columns(j)]))

    def local_states(j, ext):
        cols = columns(j)
        spread_to = spreader(j)
        tap_rows, bias = 0.5 * tapx_ref[:, cols], 0.5 * biasx_ref[:, cols]
        for s in range(2):
            rows_at = mm(r_row[s], spread_to)
            state = None
            for g in range(groups) if s == 0 else range(groups - 1, -1, -1):
                rows = slice(g * GROUP, (g + 1) * GROUP)
                x = conv(ext, s, g, tap_rows, bias)
                x_buf[s, rows, cols] = x.astype(bf)
                xs = (x * mm(g_col[s, rows], spread_to)).astype(bf)
                xs_buf[s, rows, cols] = xs
                fresh = mm(bt_buf[s, g], xs)
                for p in (0, 1) if s == 0 else (1, 0):
                    c = 2 * g + p
                    part = fresh[p * states : (p + 1) * states]
                    if state is None:
                        st_buf[s, c, :, cols] = jnp.zeros((states, BLOCK), bf)
                        state = rows_at[c : c + 1] * part
                    else:
                        st_buf[s, c, :, cols] = state.astype(bf)
                        state = rows_at[c : c + 1] * (state + part)
            for p in range(2):
                lanes = slice(p * half, (p + 1) * half)
                put(loc, j * 2 + p, s, state[:, lanes], rows_at[8:9, lanes])
        core_copy(j).start()

    def two_blocks(i, _):
        j = 2 * i
        wx_load(j + 1).wait()
        exchange(j)
        project_x(j + 1, ext_odd)
        local_states(j, ext_even)
        wx_load(j + 2).wait()
        exchange(j + 1)
        project_x(j + 2, ext_even)
        local_states(j + 1, ext_odd)
        return 0

    wx_load(0).wait()
    spread_rows(ext_odd, mm(a_buf[...], wbc_buf[...]))
    project_x(0, ext_even)
    for s in range(2):
        keep = same & older[s]
        for g in range(groups):
            rows = slice(g * GROUP, (g + 1) * GROUP)
            both = conv(ext_odd, s, g, 0.5 * tapbc_ref[...], 0.5 * biasbc_ref[...])
            b, c = both[:, :states].astype(bf), both[:, states:].astype(bf)
            lh_buf[s, rows, 0:states] = c
            lh_buf[s, rows, states : states + GROUP] = jnp.where(keep, nt(c, b), 0.0).astype(bf)
            bt = b.astype(f32).T
            lower = r < SUB
            bt_buf[s, g, 0:states] = jnp.where(lower, bt, 0.0).astype(bf)
            bt_buf[s, g, states : 2 * states] = jnp.where(lower, 0.0, bt).astype(bf)

    lax.fori_loop(0, blocks // 2 - 1, two_blocks, 0)
    wx_load(blocks - 1).wait()
    wz_load.start()
    exchange(jnp.int32(blocks - 2))
    project_x(blocks - 1, ext_odd)
    local_states(blocks - 2, ext_even)
    wo_load.start()
    exchange(jnp.int32(blocks - 1))
    local_states(blocks - 1, ext_odd)

    def local_outputs(j, _):
        @pl.when((j == 0) | (j == 2) | (j == 5))
        def _():
            exchange(blocks + (j + 1) // 3)

        cols = columns(j)
        spread_to = spreader(j)
        for s in range(2):
            skip = mm(r_row[s], spread_to)[9:10]
            for g in range(groups):
                rows = slice(g * GROUP, (g + 1) * GROUP)
                factor = mm(f_col[s, rows], spread_to)
                xs = xs_buf[s, rows, cols]
                x = x_buf[s, rows, cols].astype(f32)
                ys = []
                for p in range(2):
                    c = 2 * g + p
                    rhs = jnp.concatenate([st_buf[s, c, :, cols], xs], axis=0)
                    ys.append(mm(lh_buf[s, c * SUB : (c + 1) * SUB], rhs))
                y = jnp.concatenate(ys, axis=0) * factor + skip * x
                x_buf[s, rows, cols] = y.astype(bf)
        return 0

    lax.fori_loop(0, blocks, local_outputs, 0)

    wz_load.wait()

    def gates(j, _):
        @pl.when((j % 2 == 0) & (j < 8))
        def _():
            exchange(blocks + 3 + j // 2)

        cols = columns(j)
        h = 0.5 * mm(a_buf[HALO : HALO + 2 * length], wz_buf[:, cols])
        z = (h + h * jnp.tanh(h)).astype(bf)
        for s in range(2):
            xs_buf[s, :, cols] = z[s * length : (s + 1) * length]
        return 0

    lax.fori_loop(0, blocks, gates, 0)
    for at in range(blocks + 7, blocks + lines + 3):
        exchange(jnp.int32(at))
    for b in range(blocks):
        ent_arrived(b).wait_recv()
    wo_load.wait()

    def y_copy(i):
        return send(y_out.at[i], y_in.at[i], y_s.at[i], y_r.at[i], chan=other_chan)

    part = feats // 2

    def rows_out(i, _):
        rows = pl.ds(pl.multiple_of(i * GROUP, GROUP), GROUP)

        def gate(j):
            cols = columns(j)
            spread_to = spreader(j)
            total = 0.0
            for s in range(2):
                carried = mm(lh_buf[s, rows, 0:states], entry[j, s])
                y = x_buf[s, rows, cols].astype(f32) + carried * mm(e_col[s, rows], spread_to)
                total = total + y * xs_buf[s, rows, cols].astype(f32)
            gated[:, cols] = total.astype(bf)

        def two_gates(n, _):
            gate(2 * n)
            gate(2 * n + 1)
            return 0

        lax.fori_loop(0, blocks // 2, two_gates, 0)

        def project(chan, target, p):
            cols = pl.ds(pl.multiple_of(chan * feats + p * part, BLOCK), part)
            target[2 * i + p] = mm(gated[...], w_buf[:, cols]).astype(bf)

        for p in range(2):
            project(other_chan, y_out, p)
            y_copy(2 * i + p).start()
        for p in range(2):
            project(lane_mate, own, p)
        return 0

    lax.fori_loop(0, groups, rows_out, 0)

    for i in range(2 * groups):
        y_copy(i).wait_recv()
        rows = slice(i // 2 * GROUP, (i // 2 + 1) * GROUP)
        cols = slice(i % 2 * part, (i % 2 + 1) * part)
        out_ref[cols, rows] = (own[i].astype(f32) + y_in[i].astype(f32)).T.astype(bf)

    for i in range(2 * groups):
        y_copy(i).wait_send()
    for b in range(blocks):
        core_copy(b).wait_send()
        x_copy(b).wait_send()
        ent_copy(b).wait_send()

    @pl.when(line < lines - 1)
    def _():
        for b in range(blocks):
            z_copy(b, 0).wait_send()

    @pl.when(line > 0)
    def _():
        for b in range(blocks):
            z_copy(b, 1).wait_send()


def fused_device(
    hidden, nucleotides, base_embed, x_proj, gate_proj, bc_proj, conv_x, bias_x, conv_bc,
    bias_bc, log_decay, d_skip, out_proj,
):
    length, depth = hidden.shape[1:]
    inner = x_proj.shape[1]
    feats = out_proj.shape[1] // 2
    heads = d_skip.shape[0]
    states = conv_bc.shape[1] // 2
    blocks, groups, subs, half = inner // BLOCK, length // GROUP, length // SUB, BLOCK // 2
    rows = 2 * length + 2 * HALO
    bf, f32 = jnp.bfloat16, jnp.float32
    vmem, dma = pltpu.VMEM, pltpu.SemaphoreType.DMA
    small = pl.BlockSpec(memory_space=pltpu.VMEM)
    large = pl.BlockSpec(memory_space=pl.ANY)
    pair = (blocks, 2, states + PAD, half)
    out = pl.pallas_call(
        functools.partial(layer_kernel, inner // heads),
        out_shape=jax.ShapeDtypeStruct((feats, length), bf),
        in_specs=[small, large, small, large, large, large, large] + [small] * 6,
        out_specs=small,
        scratch_shapes=[
            vmem((rows, depth), bf),
            vmem((depth, inner), bf),
            vmem((depth, inner), bf),
            vmem((depth, 2 * states), bf),
            vmem((2, rows, BLOCK // 2), f32),
            vmem((2, rows, BLOCK // 2), f32),
            vmem((2, length, inner), bf),
            vmem((2, length, inner), bf),
            vmem((2, subs, states, inner), bf),
            vmem((2, length, states + GROUP), bf),
            vmem((2, groups, 2 * states, GROUP), bf),
            vmem((2, length, 2 * heads), bf),
            vmem((2, length, 2 * heads), bf),
            vmem((2, length, 2 * heads), bf),
            vmem((2, 16, 2 * heads), bf),
            vmem((1, length), jnp.int32),
            vmem((1, length), jnp.int32),
            vmem((2 * blocks, 2, states + PAD, half), bf),
            vmem(pair, bf),
            vmem(pair, bf),
            vmem(pair, bf),
            vmem((blocks, 2, states, half), f32),
            vmem((blocks, 2, 8, half), f32),
            vmem((blocks, 2, states, half), bf),
            vmem((blocks, 2, states, half), bf),
            vmem((blocks, 2, states, half), bf),
            vmem((blocks, 2, states, BLOCK), bf),
            vmem((GROUP, inner), bf),
            vmem((2 * groups, GROUP, feats // 2), bf),
            vmem((2 * groups, GROUP, feats // 2), bf),
            vmem((2 * groups, GROUP, feats // 2), bf),
            dma((5,)), dma((blocks,)), dma((4,)), dma((4,)),
            dma((blocks,)), dma((blocks,)), dma((blocks,)), dma((blocks,)),
            dma((blocks, 2)), dma((blocks, 2)), dma((blocks,)), dma((blocks,)),
            dma((2 * groups,)), dma((2 * groups,)),
        ],
        compiler_params=pltpu.CompilerParams(
            collective_id=0, has_side_effects=True, vmem_limit_bytes=67043328
        ),
        name="layer",
    )(
        nucleotides[None], hidden, base_embed, x_proj, gate_proj, bc_proj, out_proj, conv_x, bias_x[None], conv_bc,
        bias_bc[None], log_decay, d_skip[None],
    )
    return out


def any_device(*args):
    hidden, x_proj, conv_bc = args[0], args[3], args[8]
    fits = lax.axis_size("chan") == 2 and lax.axis_size("seq") % 4 == 0 and lax.axis_size("seq") >= 8
    fits = fits and hidden.shape[1] == 8 * SUB and conv_bc.shape[1] == BLOCK
    fits = fits and x_proj.shape[1] % (2 * BLOCK) == 0 and x_proj.shape[1] >= 8 * BLOCK
    return fused_device(*args) if fits else per_device(*args)


def solution(mesh):
    in_specs = (
        P(None, "seq", None), P("seq"), P(), P(None, "chan"), P(None, "chan"), P(),
        P(None, "chan"), P("chan"), P(), P(), P(None, "chan", "seq"), P("chan"), P("chan", None),
    )
    return jax.shard_map(
        any_device, mesh=mesh, in_specs=in_specs, out_specs=P("chan", "seq"), check_vma=False
    )
```
